32 devices in a mesh: gx: 4 (over y, x), gy: 4 (over z), gz: 2 (over core).
Axes of the slice: x: 2, y: 2, z: 4, core: 2. Of those that a mesh axis runs over, the one named last changes fastest.
Arguments:
- state: float32 [3, 32, 160, 512], P(None, 'gz', 'gy', 'gx'), may hold values from -6 to 6
- right_side: float32 [3, 32, 160, 512], P(None, 'gz', 'gy', 'gx'), may hold values from -6 to 6
- permeability: bfloat16 [32, 160, 512], P('gz', 'gy', 'gx'), may hold values from 0.099609375 to 10
- pore_volume: bfloat16 [32, 160, 512], P('gz', 'gy', 'gx'), may hold values from 0.019897461 to 0.19921875
- facies: int32 [32], P('gz'), may hold values from 0 to 3
- storage_table: float32 [4, 3, 3], replicated, may hold values from -0.3 to 2, as said below
- coupling_table: float32 [4, 3, 3], replicated, may hold values from -0.3 to 2, as said below
Outputs:
- new_state: float32 [3, 32, 160, 512], P(None, 'gz', 'gy', 'gx')
- correction: float32 [160, 512], P('gy', 'gx')
The draws below stay inside these ranges and needn't reach their ends.
Inputs may be any that keep to these rules, and one draw needn't show every extreme that they name: `storage_table`: each facies block has a diagonal of 1 to 2 and off-diagonal entries of magnitude at most 0.3. `coupling_table`: each facies block has a diagonal of 1 to 2 and off-diagonal entries of magnitude at most 0.3.
All inputs are finite; a program needn't handle non-finite values.
Results may differ from the reference program's by a relative error of at most 0.0003.
Values sent between devices are 32-bit elements; how exact they have to be, the bound alone decides.
A program may use at most 64 MiB of HBM per device.

```python
import math
import jax
import jax.numpy as jnp
from jax import lax

FACIES = 4
SWEEPS = 8
NX = 512
NY = 160
NZ = 32


def draw_table(key):
    first_key, second_key = jax.random.split(key)
    diagonal = jax.random.uniform(first_key, (FACIES, 3), jnp.float32, 1.0, 2.0)
    spread = jax.random.uniform(second_key, (FACIES, 3, 3), jnp.float32, -0.3, 0.3)
    identity = jnp.eye(3, dtype=jnp.float32)
    return spread * (1.0 - identity) + diagonal[:, :, None] * identity


def draw_storage_table(key, part):
    return draw_table(jax.random.fold_in(key, 11))


def draw_coupling_table(key, part):
    return draw_table(jax.random.fold_in(key, 12))


def plant(result, rng, least, top_value):
    longest = result.shape.index(max(result.shape))
    spots = []
    for shift in (0, 1):
        where = [jax.random.randint(jax.random.fold_in(rng, axis), (), 0, length) for axis, length in enumerate(result.shape)]
        where[longest] = (where[longest] + shift) % result.shape[longest]
        spots.append(tuple(where))
    return result.at[spots[0]].set(least).at[spots[1]].set(top_value)


def steps_of(rng, dims, cuts, low, largest):
    factor_of, own = 1.0, jax.random.fold_in(rng, 6)
    for dim, parts in cuts:
        heights = jnp.exp(jax.random.uniform(jax.random.fold_in(own, dim), (parts,), jnp.float32, low / len(cuts), largest / len(cuts)))
        factor_of = factor_of * jnp.repeat(heights, dims[dim] // parts).reshape([-1 if axis == dim else 1 for axis in range(len(dims))])
    return factor_of


def gaussian(rng, extent, width, limit, shards=(), held_as=jnp.bfloat16):
    gain = steps_of(rng, extent, shards, -0.22, 0.18) if shards else 1.0
    result = jax.random.normal(rng, extent, jnp.float32) * width * gain
    return jnp.minimum(jnp.maximum(result, -limit), limit).astype(held_as)


def setup_inputs(seed: int = 0) -> dict:
    arg_keys = jax.random.split(jax.random.key(seed), 8)
    state = gaussian(arg_keys[0], (3, NZ, NY, NX), 1.0, 6.0, ((1, 2), (2, 4), (3, 4)), jnp.float32)
    right_side = gaussian(arg_keys[1], (3, NZ, NY, NX), 1.0, 6.0, ((1, 2), (2, 4), (3, 4)), jnp.float32)
    permeability = jnp.clip(jnp.exp(math.log(10.0) - 4.609084 * jax.random.uniform(arg_keys[2], (NZ, NY, NX), jnp.float32) ** steps_of(arg_keys[2], (NZ, NY, NX), ((0, 2), (1, 4), (2, 4)), -0.2, 0.2)), 0.099609375, 10.0).astype(jnp.bfloat16)
    pore_volume = jnp.clip(jnp.exp(math.log(0.19921875) - 2.3038113 * jax.random.uniform(arg_keys[3], (NZ, NY, NX), jnp.float32) ** steps_of(arg_keys[3], (NZ, NY, NX), ((0, 2), (1, 4), (2, 4)), -0.2, 0.2)), 0.019897461, 0.19921875).astype(jnp.bfloat16)
    facies = plant(jax.random.randint(arg_keys[4], (NZ,), 0, FACIES), jax.random.fold_in(arg_keys[4], 1), 0, FACIES - 1).astype(jnp.int32)
    storage_table = draw_storage_table(jax.random.fold_in(arg_keys[7], 71), 0)
    coupling_table = draw_coupling_table(jax.random.fold_in(arg_keys[7], 71), 0)
    return dict(state=state, right_side=right_side, permeability=permeability, pore_volume=pore_volume, facies=facies, storage_table=storage_table, coupling_table=coupling_table)


relax = 0.8


def layer_tables(facies, table):
    onehot = (facies[:, None] == jnp.arange(table.shape[0])[None, :]).astype(jnp.float32)
    return jnp.dot(onehot, table.reshape(table.shape[0], 9), precision=lax.Precision.HIGHEST)


def layer_coefficient(rows, row_index, column_index):
    return rows[:, 3 * row_index + column_index][:, None, None]


def neighbours(padded):
    return [padded[..., 2:, 1:-1, 1:-1], padded[..., :-2, 1:-1, 1:-1],
            padded[..., 1:-1, 2:, 1:-1], padded[..., 1:-1, :-2, 1:-1],
            padded[..., 1:-1, 1:-1, 2:], padded[..., 1:-1, 1:-1, :-2]]


def face_weights(padded_perm):
    center = padded_perm[1:-1, 1:-1, 1:-1]
    return [2.0 * center * nearby / (center + nearby) for nearby in neighbours(padded_perm)]


def apply_operator(padded_state, weights, storage, storage_rows, coupling_rows):
    center = padded_state[:, 1:-1, 1:-1, 1:-1]
    fluxes = jnp.zeros_like(center)
    for weight, nearby in zip(weights, neighbours(padded_state)):
        fluxes = fluxes + weight[None] * (center - nearby)
    outputs = []
    for row_index in range(3):
        local = sum(layer_coefficient(storage_rows, row_index, k) * center[k] for k in range(3))
        moved = sum(layer_coefficient(coupling_rows, row_index, k) * fluxes[k] for k in range(3))
        outputs.append(storage * local + moved)
    return jnp.stack(outputs)


def coarse_planes(residual, weights, storage, storage_rows, coupling_rows):
    first_coupling = layer_coefficient(coupling_rows, 0, 0)
    first_storage = layer_coefficient(storage_rows, 0, 0)
    items = [residual[0], storage * first_storage] + [weights[k] * first_coupling for k in range(2, 6)]
    return jnp.stack([jnp.sum(item, axis=0) for item in items])


def jacobi(field, bordered, planes):
    diagonal = planes[1] + planes[2] + planes[3] + planes[4] + planes[5]
    nearby = (planes[2] * bordered[2:, 1:-1] + planes[3] * bordered[:-2, 1:-1]
              + planes[4] * bordered[1:-1, 2:] + planes[5] * bordered[1:-1, :-2])
    return field + relax * (planes[0] - diagonal * field + nearby) / diagonal


def block_solve(weights, storage, storage_rows, coupling_rows, residual):
    face_total = weights[0] + weights[1] + weights[2] + weights[3] + weights[4] + weights[5]
    entries = [[storage * layer_coefficient(storage_rows, r, c) + face_total * layer_coefficient(coupling_rows, r, c)
                for c in range(3)] for r in range(3)]

    def cofactor(r, c):
        return (entries[(r + 1) % 3][(c + 1) % 3] * entries[(r + 2) % 3][(c + 2) % 3]
                - entries[(r + 1) % 3][(c + 2) % 3] * entries[(r + 2) % 3][(c + 1) % 3])

    factors = [[cofactor(r, c) for c in range(3)] for r in range(3)]
    determinant = entries[0][0] * factors[0][0] + entries[0][1] * factors[0][1] + entries[0][2] * factors[0][2]
    return jnp.stack([(factors[0][r] * residual[0] + factors[1][r] * residual[1] + factors[2][r] * residual[2]) / determinant
                      for r in range(3)])


def reference(state, right_side, permeability, pore_volume, facies, storage_table, coupling_table):
    perm_wide = permeability.astype(jnp.float32)
    storage = pore_volume.astype(jnp.float32)
    storage_rows = layer_tables(facies, storage_table)
    coupling_rows = layer_tables(facies, coupling_table)
    weights = face_weights(jnp.pad(perm_wide, 1))
    widths = ((0, 0), (1, 1), (1, 1), (1, 1))
    residual = right_side - apply_operator(jnp.pad(state, widths), weights, storage, storage_rows, coupling_rows)
    planes = coarse_planes(residual, weights, storage, storage_rows, coupling_rows)
    correction = jnp.zeros(planes.shape[1:], jnp.float32)
    for repeat_index in range(SWEEPS):
        correction = jacobi(correction, jnp.pad(correction, 1), planes)
    state_one = state.at[0].add(correction[None])
    later_residual = right_side - apply_operator(jnp.pad(state_one, widths), weights, storage, storage_rows, coupling_rows)
    new_state = state_one + block_solve(weights, storage, storage_rows, coupling_rows, later_residual)
    return new_state, correction
```

```python
import functools
import jax
import jax.numpy as jnp
from jax import lax
from jax.experimental import pallas as pl
from jax.experimental.pallas import tpu as pltpu
from jax.sharding import PartitionSpec as P

SWEEPS = 8
RELAX = 0.8
MESH = pl.DeviceIdType.MESH
HALO = 8
LANES = 128

PLANES = 4
SIDES = [(-1, 0), (1, 0), (0, -1), (0, 1), (-1, -1), (-1, 1), (1, -1), (1, 1)]


def face(a, b):
    return 2.0 * a * b / (a + b)


def kernel(sizes, facies, mtab, ktab, state_hbm, rhs_hbm, perm_hbm, pore_hbm,
           new_hbm, corr_ref,
           u, rhs, permb, poreb, ysend, yrecv, xsend, xrecv,
           flux, ty, txp, txm, tzs, tot, w, qv, zplanes, ext, cxsend, cxrecv, field,
           in_sem, out_sem, h_send, h_recv, z_send, z_recv, c_send, c_recv):
    ngx, ngy, ngz, nz, ny, nx = sizes
    ix, iy, iz = lax.axis_index("gx"), lax.axis_index("gy"), lax.axis_index("gz")
    own = slice(HALO, HALO + ny)

    loads = [
        pltpu.make_async_copy(perm_hbm, permb, in_sem.at[0]),
        pltpu.make_async_copy(state_hbm, u.at[0:3, 1:nz + 1, own], in_sem.at[1]),
        pltpu.make_async_copy(pore_hbm, poreb, in_sem.at[2]),
        pltpu.make_async_copy(rhs_hbm, rhs, in_sem.at[3]),
    ]
    for load in loads:
        load.start()

    def exists(dy, dx):
        ok = None
        for d, i, n in ((dy, iy, ngy), (dx, ix, ngx)):
            if d:
                here = (i > 0) if d < 0 else (i < n - 1)
                ok = here if ok is None else jnp.logical_and(ok, here)
        return ok

    def at(dy, dx):
        return {"gx": ix + dx, "gy": iy + dy, "gz": iz}

    barrier = pltpu.get_barrier_semaphore()
    for side in SIDES:
        @pl.when(exists(*side))
        def _(side=side):
            pl.semaphore_signal(barrier, inc=1, device_id=at(*side), device_id_type=MESH)
    for d in range(1, ngz):
        pl.semaphore_signal(barrier, inc=1, device_id={"gx": ix, "gy": iy, "gz": lax.rem(iz + d, ngz)},
                            device_id_type=MESH)

    lane = lax.broadcasted_iota(jnp.int32, (ny, nx), 1)

    def zero(ref):
        ref[...] = jnp.zeros(ref.shape, ref.dtype)

    for cond, refs in (
        (iz == 0, [u.at[:, 0, own]]),
        (iz == ngz - 1, [u.at[:, nz + 1, own]]),
        (iy == 0, [yrecv.at[0], ext.at[:, 0:HALO]]),
        (iy == ngy - 1, [yrecv.at[1], ext.at[:, HALO + ny:]]),
        (ix == 0, [xrecv.at[0], cxrecv.at[0, own]]),
        (ix == ngx - 1, [xrecv.at[1], cxrecv.at[1, own]]),
        (jnp.logical_or(iy == 0, ix == 0), [cxrecv.at[0, 0:HALO]]),
        (jnp.logical_or(iy == 0, ix == ngx - 1), [cxrecv.at[1, 0:HALO]]),
        (jnp.logical_or(iy == ngy - 1, ix == 0), [cxrecv.at[0, HALO + ny:]]),
        (jnp.logical_or(iy == ngy - 1, ix == ngx - 1), [cxrecv.at[1, HALO + ny:]]),
    ):
        @pl.when(cond)
        def _(refs=refs):
            for ref in refs:
                zero(ref)
    zero(field)

    loads[0].wait()

    def widen(z, _):
        u[3, z + 1, own, :] = permb[z].astype(jnp.float32)
        return 0

    lax.fori_loop(0, nz, widen, 0)
    loads[1].wait()

    def pack(z, packed):
        for k in range(4):
            slab = u[k, z + 1, own, :]
            j = k * nz + z
            ysend[0, pl.ds(j, 1), :] = u[k, z + 1, HALO:HALO + 1, :]
            ysend[1, pl.ds(j, 1), :] = u[k, z + 1, HALO + ny - 1:HALO + ny, :]
            packed = jnp.where(lax.shift_right_logical(lane, 1) == j,
                               pltpu.roll(slab, lax.rem(2 * j + 1, nx), 1), packed)
        return packed

    xsend[...] = lax.fori_loop(0, nz, pack, jnp.zeros((ny, nx), jnp.float32))

    count = sum(exists(*side).astype(jnp.int32) for side in SIDES) + (ngz - 1)
    pl.semaphore_wait(barrier, count)

    def remote(src, dst, send, recv, device):
        return pltpu.make_async_remote_copy(src_ref=src, dst_ref=dst, send_sem=send, recv_sem=recv,
                                            device_id=device, device_id_type=MESH)

    def z_device(d):
        return {"gx": ix, "gy": iy, "gz": iz + d}

    halos = [
        (iz < ngz - 1, iz > 0, remote(u.at[:, nz, own], u.at[:, 0, own], h_send.at[0], h_recv.at[0], z_device(1))),
        (iz > 0, iz < ngz - 1, remote(u.at[:, 1, own], u.at[:, nz + 1, own], h_send.at[1], h_recv.at[1], z_device(-1))),
        (exists(1, 0), exists(-1, 0), remote(ysend.at[1], yrecv.at[0], h_send.at[2], h_recv.at[2], at(1, 0))),
        (exists(-1, 0), exists(1, 0), remote(ysend.at[0], yrecv.at[1], h_send.at[3], h_recv.at[3], at(-1, 0))),
        (exists(0, 1), exists(0, -1), remote(xsend, xrecv.at[0], h_send.at[4], h_recv.at[4], at(0, 1))),
        (exists(0, -1), exists(0, 1), remote(xsend, xrecv.at[1], h_send.at[5], h_recv.at[5], at(0, -1))),
    ]

    def start(copies):
        for sends, _, copy in copies:
            @pl.when(sends)
            def _(copy=copy):
                copy.start()

    def wait_recv(copies):
        for _, gets, copy in copies:
            @pl.when(gets)
            def _(copy=copy):
                copy.wait_recv()

    def wait_send(copies):
        for sends, _, copy in copies:
            @pl.when(sends)
            def _(copy=copy):
                copy.wait_send()

    start(halos[4:])
    start(halos[2:4])
    start(halos[:2])
    loads[2].wait()
    loads[3].wait()
    wait_recv(halos)

    left = xrecv[0]
    border = jnp.where(lax.rem(lane, 2) == 0, left, pltpu.roll(xrecv[1], nx - 2, 1))
    mine = pltpu.roll(xsend[...], nx - 1, 1)
    left_t = jnp.where(lane >= 6 * nz, face(jnp.where(lane >= 6 * nz, left, 1.0), jnp.where(lane >= 6 * nz, mine, 1.0)), 0.0)
    first, last = lane == 0, lane == nx - 1

    def coefficient(table, z, r, c):
        return table[facies[z], r, c]

    def assemble(z, carry):
        tzm, s_rhs, s_diag, s_ty, s_tx = carry
        for k in range(4):
            j = k * nz + z
            u[k, z + 1, HALO - 1:HALO, :] = yrecv[0, pl.ds(j, 1), :]
            u[k, z + 1, HALO + ny:HALO + ny + 1, :] = yrecv[1, pl.ds(j, 1), :]

        def around(k):
            c = u[k, z + 1, own, :]
            h = pltpu.roll(border, lax.rem(2 * nx - 2 * (k * nz + z), nx), 1)
            return (c, u[k, z + 2, own, :], u[k, z, own, :],
                    u[k, z + 1, HALO + 1:HALO + ny + 1, :], u[k, z + 1, HALO - 1:HALO + ny - 1, :],
                    jnp.where(last, h, pltpu.roll(c, nx - 1, 1)), jnp.where(first, h, pltpu.roll(c, 1, 1)))

        q, qzp, _, qyp, _, qxp, _ = around(3)
        tzp = face(q, qzp)
        typ = face(q, qyp)
        ty[z, own, :] = typ
        ty[z, HALO - 1:HALO, :] = face(u[3, z + 1, HALO - 1:HALO, :], u[3, z + 1, HALO:HALO + 1, :])
        tym = ty[z, HALO - 1:HALO + ny - 1, :]
        xp = face(q, qxp)
        xm = jnp.where(first, pltpu.roll(left_t, lax.rem(2 * nx - 2 * (3 * nz + z), nx), 1), pltpu.roll(xp, 1, 1))
        txp[z] = xp
        txm[z] = xm
        tz = tzp + tzm
        areal = typ + tym + xp + xm
        tzs[z] = tz
        tot[z] = tz + areal
        v = poreb[z].astype(jnp.float32)
        local, moved = 0.0, 0.0
        for k in range(3):
            c, zp, zm, yp, ym, cxp, cxm = around(k)
            f = (tzp * (c - zp) + tzm * (c - zm) + typ * (c - yp) + tym * (c - ym)
                 + xp * (c - cxp) + xm * (c - cxm))
            flux[k, z] = f
            local = local + coefficient(mtab, z, 0, k) * c
            moved = moved + coefficient(ktab, z, 0, k) * f
        res = rhs[0, z] - (v * local + moved)
        rhs[0, z] = res
        k00 = coefficient(ktab, z, 0, 0)
        return (tzp, s_rhs + res, s_diag + (v * coefficient(mtab, z, 0, 0) + k00 * areal),
                s_ty + k00 * typ, s_tx + k00 * xp)

    nil = jnp.zeros((ny, nx), jnp.float32)
    carry = lax.fori_loop(0, nz, assemble, (face(u[3, 1, own, :], u[3, 0, own, :]), nil, nil, nil, nil))
    for p in range(PLANES):
        zplanes[iz, p] = carry[p + 1]

    others = [lax.rem(iz + d, ngz) for d in range(1, ngz)]
    sums = [remote(zplanes.at[iz], zplanes.at[iz], z_send.at[d], z_recv.at[iz], {"gx": ix, "gy": iy, "gz": peer})
            for d, peer in enumerate(others)]
    for copy in sums:
        copy.start()

    def solve(z, _):
        v = poreb[z].astype(jnp.float32)
        total = tot[z]
        m = [[coefficient(mtab, z, r, c) for c in range(3)] for r in range(3)]
        kk = [[coefficient(ktab, z, r, c) for c in range(3)] for r in range(3)]
        e = [[v * m[r][c] + total * kk[r][c] for c in range(3)] for r in range(3)]

        def cofactor(r, c):
            return (e[(r + 1) % 3][(c + 1) % 3] * e[(r + 2) % 3][(c + 2) % 3]
                    - e[(r + 1) % 3][(c + 2) % 3] * e[(r + 2) % 3][(c + 1) % 3])

        cells = [u[k, z + 1, own, :] for k in range(3)]
        f = [flux[k, z] for k in range(3)]
        res = [rhs[0, z]]
        for r in (1, 2):
            res.append(rhs[r, z] - (v * (m[r][0] * cells[0] + m[r][1] * cells[1] + m[r][2] * cells[2])
                                    + (kk[r][0] * f[0] + kk[r][1] * f[1] + kk[r][2] * f[2])))
        fac = [[cofactor(r, c) for c in range(3)] for r in range(3)]
        inv = 1.0 / (e[0][0] * fac[0][0] + e[0][1] * fac[0][1] + e[0][2] * fac[0][2])
        for r in range(3):
            w[r, z] = cells[r] + (fac[0][r] * res[0] + fac[1][r] * res[1] + fac[2][r] * res[2]) * inv
            qv[r, z] = (fac[0][r] * kk[0][0] + fac[1][r] * kk[1][0] + fac[2][r] * kk[2][0]) * inv
        return 0

    half = nz // 4
    lax.fori_loop(0, half, solve, 0)

    for peer in others:
        remote(zplanes.at[peer], zplanes.at[peer], z_send.at[0], z_recv.at[peer],
               {"gx": ix, "gy": iy, "gz": peer}).wait_recv()
    packed = nil
    for p in range(PLANES):
        plane = zplanes[0, p]
        for i in range(1, ngz):
            plane = plane + zplanes[i, p]
        ext[p, own, :] = plane
        packed = jnp.where(lax.shift_right_logical(lane, 4) == p, pltpu.roll(plane, 2 * HALO * p + HALO, 1), packed)
    cxsend[...] = packed

    low, high = slice(0, HALO), slice(ny - HALO, ny)
    elow, ehigh = slice(0, HALO), slice(HALO + ny, 2 * HALO + ny)
    coarse = []
    for s, (dy, dx) in enumerate(SIDES):
        rows = low if dy < 0 else high
        into = ehigh if dy < 0 else elow
        if dx == 0:
            src, dst = ext.at[:, slice(rows.start + HALO, rows.stop + HALO)], ext.at[:, into]
        elif dy == 0:
            src, dst = cxsend, cxrecv.at[0 if dx > 0 else 1, own]
        else:
            src, dst = cxsend.at[rows], cxrecv.at[0 if dx > 0 else 1, into]
        coarse.append((exists(dy, dx), exists(-dy, -dx), remote(src, dst, c_send.at[s], c_recv.at[s], at(dy, dx))))
    start(coarse)
    lax.fori_loop(half, nz, solve, 0)
    wait_recv(coarse)

    rows = ny + 2 * HALO
    elane = lax.broadcasted_iota(jnp.int32, (rows, nx), 1)
    efirst, elast = elane == 0, elane == nx - 1
    near = jnp.logical_or(elane < HALO, elane >= nx - HALO)
    beside = jnp.where(lax.rem(elane, 2 * HALO) < HALO, cxrecv[0], cxrecv[1])
    a = [ext[p] for p in range(PLANES)]
    b = [jnp.where(near, pltpu.roll(beside, nx - (2 * HALO * p + HALO), 1), 0.0) for p in range(PLANES)]

    def east(a, b):
        ra, rb = pltpu.roll(a, nx - 1, 1), pltpu.roll(b, nx - 1, 1)
        return jnp.where(elast, rb, ra), jnp.where(elast, ra, rb)

    def west(a, b):
        ra, rb = pltpu.roll(a, 1, 1), pltpu.roll(b, 1, 1)
        return jnp.where(efirst, rb, ra), jnp.where(efirst, ra, rb)

    mid = slice(HALO, HALO + rows)
    wests = west(a[3], b[3])
    terms = []
    for s, planes in enumerate((a, b)):
        there = planes[1] > 0.0
        inv = jnp.where(there, RELAX / jnp.where(there, planes[1], 1.0), 0.0)
        field[s, mid, :] = planes[2]
        south = field[s, HALO - 1:HALO - 1 + rows, :]
        terms.append((planes[0] * inv, planes[2] * inv, south * inv, planes[3] * inv, wests[s] * inv))

    c = [terms[0][0], terms[1][0]]
    for sweep in range(1, SWEEPS):
        e, ws = east(*c), west(*c)
        for s in range(2):
            field[s, mid, :] = c[s]
        nxt = []
        for s in range(2):
            r, tyn, tys, txe, txw = terms[s]
            nxt.append((1.0 - RELAX) * c[s] + r
                       + tyn * field[s, HALO + 1:HALO + 1 + rows, :] + tys * field[s, HALO - 1:HALO - 1 + rows, :]
                       + txe * e[s] + txw * ws[s])
        c = nxt
    e, ws = east(*c), west(*c)
    field[0, mid, :] = c[0]
    field[1, mid, :] = e[0]
    base = 2 * HALO
    ce = field[1, base:base + ny, :]
    field[1, mid, :] = ws[0]
    cw = field[1, base:base + ny, :]
    cc = field[0, base:base + ny, :]
    cn, cs = field[0, base + 1:base + 1 + ny, :], field[0, base - 1:base - 1 + ny, :]
    corr_ref[...] = cc

    def finish(z, _):
        g = (tzs[z] * cc + ty[z, own, :] * cn + ty[z, HALO - 1:HALO + ny - 1, :] * cs
             + txp[z] * ce + txm[z] * cw)
        for r in range(3):
            w[r, z] = w[r, z] + qv[r, z] * g
        return 0

    parts = 4
    step = nz // parts
    outs = []
    for part in range(parts):
        lax.fori_loop(part * step, (part + 1) * step, finish, 0)
        chunk = slice(part * step, (part + 1) * step)
        outs.append(pltpu.make_async_copy(w.at[:, chunk], new_hbm.at[:, chunk], out_sem.at[part]))
        outs[-1].start()
    wait_send(halos)
    for copy in sums:
        copy.wait_send()
    wait_send(coarse)
    for copy in outs:
        copy.wait()


def per_device(sizes, state, right_side, permeability, pore_volume, facies, storage_table, coupling_table):
    _, nz, ny, nx = state.shape
    sizes = sizes + (nz, ny, nx)
    f32 = jnp.float32
    ngz = sizes[2]
    cells = (nz, ny, nx)
    vmem = lambda *shape: pltpu.VMEM(shape, f32)
    anywhere = pl.BlockSpec(memory_space=pl.ANY)
    smem = pl.BlockSpec(memory_space=pltpu.SMEM)
    dma = lambda n: pltpu.SemaphoreType.DMA((n,))
    ey = ny + 2 * HALO
    return tuple(pl.pallas_call(
        functools.partial(kernel, sizes),
        out_shape=(jax.ShapeDtypeStruct(state.shape, f32), jax.ShapeDtypeStruct((ny, nx), f32)),
        in_specs=[smem, smem, smem, anywhere, anywhere, anywhere, anywhere],
        out_specs=(anywhere, pl.BlockSpec(memory_space=pltpu.VMEM)),
        scratch_shapes=[
            vmem(4, nz + 2, ey, nx), vmem(3, *cells),
            pltpu.VMEM(cells, permeability.dtype), pltpu.VMEM(cells, pore_volume.dtype),
            vmem(2, 4 * nz, nx), vmem(2, 4 * nz, nx), vmem(ny, nx), vmem(2, ny, nx),
            vmem(3, *cells), vmem(nz, ey, nx), vmem(*cells), vmem(*cells), vmem(*cells), vmem(*cells),
            vmem(3, *cells), vmem(3, *cells), vmem(ngz, PLANES, ny, nx), vmem(PLANES, ey, nx),
            vmem(ny, nx), vmem(2, ey, nx), vmem(2, ey + 2 * HALO, nx),
            dma(4), dma(4), dma(6), dma(6), dma(max(ngz - 1, 1)), dma(ngz), dma(8), dma(8),
        ],
        compiler_params=pltpu.CompilerParams(collective_id=0, has_side_effects=True),
        name="cpr_apply",
    )(facies, storage_table, coupling_table, state, right_side, permeability, pore_volume))


def solution(mesh):
    sizes = (mesh.shape["gx"], mesh.shape["gy"], mesh.shape["gz"])
    return jax.shard_map(
        functools.partial(per_device, sizes),
        mesh=mesh,
        in_specs=(
            P(None, "gz", "gy", "gx"),
            P(None, "gz", "gy", "gx"),
            P("gz", "gy", "gx"),
            P("gz", "gy", "gx"),
            P("gz"),
            P(),
            P(),
        ),
        out_specs=(P(None, "gz", "gy", "gx"), P("gy", "gx")),
        check_vma=False,
    )
```

```python
import functools
import jax
import jax.numpy as jnp
from jax import lax
from jax.experimental import pallas as pl
from jax.experimental.pallas import tpu as pltpu
from jax.sharding import PartitionSpec as P

SWEEPS = 8
RELAX = 0.8
MESH = pl.DeviceIdType.MESH
HALO = 8
VMEM_BYTES = 67043328

PLANES = 4
SIDES = [(-1, 0), (1, 0), (0, -1), (0, 1), (-1, -1), (-1, 1), (1, -1), (1, 1)]


def face(a, b):
    return 2.0 * a * b / (a + b)


def kernel(sizes, facies, mtab, ktab, state_hbm, rhs_hbm, perm_hbm, pore_hbm,
           w, qv, tzs, ty, txp, txm, final,
           u, rhs, permb, poreb, ysend, yrecv, xsend, xrecv,
           flux, tot, zplanes, ext, cxsend, cxrecv, field,
           in_sem, h_send, h_recv, z_send, z_recv, c_send, c_recv):
    ngx, ngy, ngz, nz, ny, nx = sizes
    ix, iy, iz = lax.axis_index("gx"), lax.axis_index("gy"), lax.axis_index("gz")
    own = slice(HALO, HALO + ny)

    loads = [
        pltpu.make_async_copy(perm_hbm, permb, in_sem.at[0]),
        pltpu.make_async_copy(state_hbm, u.at[0:3, 1:nz + 1, own], in_sem.at[1]),
        pltpu.make_async_copy(pore_hbm, poreb, in_sem.at[2]),
        pltpu.make_async_copy(rhs_hbm, rhs, in_sem.at[3]),
    ]
    for load in loads:
        load.start()

    def exists(dy, dx):
        ok = None
        for d, i, n in ((dy, iy, ngy), (dx, ix, ngx)):
            if d:
                here = (i > 0) if d < 0 else (i < n - 1)
                ok = here if ok is None else jnp.logical_and(ok, here)
        return ok

    def at(dy, dx):
        return {"gx": ix + dx, "gy": iy + dy, "gz": iz}

    barrier = pltpu.get_barrier_semaphore()
    for side in SIDES:
        @pl.when(exists(*side))
        def _(side=side):
            pl.semaphore_signal(barrier, inc=1, device_id=at(*side), device_id_type=MESH)
    for d in range(1, ngz):
        pl.semaphore_signal(barrier, inc=1, device_id={"gx": ix, "gy": iy, "gz": lax.rem(iz + d, ngz)},
                            device_id_type=MESH)

    lane = lax.broadcasted_iota(jnp.int32, (ny, nx), 1)

    def zero(ref):
        ref[...] = jnp.zeros(ref.shape, ref.dtype)

    for cond, refs in (
        (iz == 0, [u.at[:, 0, own]]),
        (iz == ngz - 1, [u.at[:, nz + 1, own]]),
        (iy == 0, [yrecv.at[0], ext.at[:, 0:HALO]]),
        (iy == ngy - 1, [yrecv.at[1], ext.at[:, HALO + ny:]]),
        (ix == 0, [xrecv.at[0], cxrecv.at[0, own]]),
        (ix == ngx - 1, [xrecv.at[1], cxrecv.at[1, own]]),
        (jnp.logical_or(iy == 0, ix == 0), [cxrecv.at[0, 0:HALO]]),
        (jnp.logical_or(iy == 0, ix == ngx - 1), [cxrecv.at[1, 0:HALO]]),
        (jnp.logical_or(iy == ngy - 1, ix == 0), [cxrecv.at[0, HALO + ny:]]),
        (jnp.logical_or(iy == ngy - 1, ix == ngx - 1), [cxrecv.at[1, HALO + ny:]]),
    ):
        @pl.when(cond)
        def _(refs=refs):
            for ref in refs:
                zero(ref)
    zero(field)

    loads[0].wait()

    def widen(z, _):
        u[3, z + 1, own, :] = permb[z].astype(jnp.float32)
        return 0

    lax.fori_loop(0, nz, widen, 0)
    loads[1].wait()

    def pack(z, packed):
        for k in range(4):
            slab = u[k, z + 1, own, :]
            j = k * nz + z
            ysend[0, pl.ds(j, 1), :] = u[k, z + 1, HALO:HALO + 1, :]
            ysend[1, pl.ds(j, 1), :] = u[k, z + 1, HALO + ny - 1:HALO + ny, :]
            packed = jnp.where(lax.shift_right_logical(lane, 1) == j,
                               pltpu.roll(slab, lax.rem(2 * j + 1, nx), 1), packed)
        return packed

    xsend[...] = lax.fori_loop(0, nz, pack, jnp.zeros((ny, nx), jnp.float32))

    count = sum(exists(*side).astype(jnp.int32) for side in SIDES) + (ngz - 1)
    pl.semaphore_wait(barrier, count)

    def remote(src, dst, send, recv, device):
        return pltpu.make_async_remote_copy(src_ref=src, dst_ref=dst, send_sem=send, recv_sem=recv,
                                            device_id=device, device_id_type=MESH)

    def z_device(d):
        return {"gx": ix, "gy": iy, "gz": iz + d}

    halos = [
        (iz < ngz - 1, iz > 0, remote(u.at[:, nz, own], u.at[:, 0, own], h_send.at[0], h_recv.at[0], z_device(1))),
        (iz > 0, iz < ngz - 1, remote(u.at[:, 1, own], u.at[:, nz + 1, own], h_send.at[1], h_recv.at[1], z_device(-1))),
        (exists(1, 0), exists(-1, 0), remote(ysend.at[1], yrecv.at[0], h_send.at[2], h_recv.at[2], at(1, 0))),
        (exists(-1, 0), exists(1, 0), remote(ysend.at[0], yrecv.at[1], h_send.at[3], h_recv.at[3], at(-1, 0))),
        (exists(0, 1), exists(0, -1), remote(xsend, xrecv.at[0], h_send.at[4], h_recv.at[4], at(0, 1))),
        (exists(0, -1), exists(0, 1), remote(xsend, xrecv.at[1], h_send.at[5], h_recv.at[5], at(0, -1))),
    ]

    def start(copies):
        for sends, _, copy in copies:
            @pl.when(sends)
            def _(copy=copy):
                copy.start()

    def wait_recv(copies):
        for _, gets, copy in copies:
            @pl.when(gets)
            def _(copy=copy):
                copy.wait_recv()

    def wait_send(copies):
        for sends, _, copy in copies:
            @pl.when(sends)
            def _(copy=copy):
                copy.wait_send()

    start(halos[4:])
    start(halos[2:4])
    start(halos[:2])
    loads[2].wait()
    loads[3].wait()
    wait_recv(halos)

    left = xrecv[0]
    border = jnp.where(lax.rem(lane, 2) == 0, left, pltpu.roll(xrecv[1], nx - 2, 1))
    mine = pltpu.roll(xsend[...], nx - 1, 1)
    left_t = jnp.where(lane >= 6 * nz, face(jnp.where(lane >= 6 * nz, left, 1.0), jnp.where(lane >= 6 * nz, mine, 1.0)), 0.0)
    first, last = lane == 0, lane == nx - 1

    def coefficient(table, z, r, c):
        return table[r, facies[z], c]

    def assemble(z, carry):
        tzm, s_rhs, s_diag, s_ty, s_tx = carry
        for k in range(4):
            j = k * nz + z
            u[k, z + 1, HALO - 1:HALO, :] = yrecv[0, pl.ds(j, 1), :]
            u[k, z + 1, HALO + ny:HALO + ny + 1, :] = yrecv[1, pl.ds(j, 1), :]

        def around(k):
            c = u[k, z + 1, own, :]
            h = pltpu.roll(border, lax.rem(2 * nx - 2 * (k * nz + z), nx), 1)
            return (c, u[k, z + 2, own, :], u[k, z, own, :],
                    u[k, z + 1, HALO + 1:HALO + ny + 1, :], u[k, z + 1, HALO - 1:HALO + ny - 1, :],
                    jnp.where(last, h, pltpu.roll(c, nx - 1, 1)), jnp.where(first, h, pltpu.roll(c, 1, 1)))

        q, qzp, _, qyp, _, qxp, _ = around(3)
        tzp = face(q, qzp)
        typ = face(q, qyp)
        ty[z, own, :] = typ
        ty[z, HALO - 1:HALO, :] = face(u[3, z + 1, HALO - 1:HALO, :], u[3, z + 1, HALO:HALO + 1, :])
        tym = ty[z, HALO - 1:HALO + ny - 1, :]
        xp = face(q, qxp)
        xm = jnp.where(first, pltpu.roll(left_t, lax.rem(2 * nx - 2 * (3 * nz + z), nx), 1), pltpu.roll(xp, 1, 1))
        txp[z] = xp
        txm[z] = xm
        tz = tzp + tzm
        areal = typ + tym + xp + xm
        tzs[z] = tz
        tot[z] = tz + areal
        v = poreb[z].astype(jnp.float32)
        local, moved = 0.0, 0.0
        for k in range(3):
            c, zp, zm, yp, ym, cxp, cxm = around(k)
            f = (tzp * (c - zp) + tzm * (c - zm) + typ * (c - yp) + tym * (c - ym)
                 + xp * (c - cxp) + xm * (c - cxm))
            flux[k, z] = f
            local = local + coefficient(mtab, z, 0, k) * c
            moved = moved + coefficient(ktab, z, 0, k) * f
        res = rhs[0, z] - (v * local + moved)
        rhs[0, z] = res
        k00 = coefficient(ktab, z, 0, 0)
        return (tzp, s_rhs + res, s_diag + (v * coefficient(mtab, z, 0, 0) + k00 * areal),
                s_ty + k00 * typ, s_tx + k00 * xp)

    nil = jnp.zeros((ny, nx), jnp.float32)
    carry = lax.fori_loop(0, nz, assemble, (face(u[3, 1, own, :], u[3, 0, own, :]), nil, nil, nil, nil))
    for p in range(PLANES):
        zplanes[iz, p] = carry[p + 1]

    others = [lax.rem(iz + d, ngz) for d in range(1, ngz)]
    sums = [remote(zplanes.at[iz], zplanes.at[iz], z_send.at[d], z_recv.at[iz], {"gx": ix, "gy": iy, "gz": peer})
            for d, peer in enumerate(others)]
    for copy in sums:
        copy.start()

    def solve(z, _):
        v = poreb[z].astype(jnp.float32)
        total = tot[z]
        m = [[coefficient(mtab, z, r, c) for c in range(3)] for r in range(3)]
        kk = [[coefficient(ktab, z, r, c) for c in range(3)] for r in range(3)]
        e = [[v * m[r][c] + total * kk[r][c] for c in range(3)] for r in range(3)]

        def cofactor(r, c):
            return (e[(r + 1) % 3][(c + 1) % 3] * e[(r + 2) % 3][(c + 2) % 3]
                    - e[(r + 1) % 3][(c + 2) % 3] * e[(r + 2) % 3][(c + 1) % 3])

        cells = [u[k, z + 1, own, :] for k in range(3)]
        f = [flux[k, z] for k in range(3)]
        res = [rhs[0, z]]
        for r in (1, 2):
            res.append(rhs[r, z] - (v * (m[r][0] * cells[0] + m[r][1] * cells[1] + m[r][2] * cells[2])
                                    + (kk[r][0] * f[0] + kk[r][1] * f[1] + kk[r][2] * f[2])))
        fac = [[cofactor(r, c) for c in range(3)] for r in range(3)]
        inv = 1.0 / (e[0][0] * fac[0][0] + e[0][1] * fac[0][1] + e[0][2] * fac[0][2])
        for r in range(3):
            w[r, z] = cells[r] + (fac[0][r] * res[0] + fac[1][r] * res[1] + fac[2][r] * res[2]) * inv
            qv[r, z] = (fac[0][r] * kk[0][0] + fac[1][r] * kk[1][0] + fac[2][r] * kk[2][0]) * inv
        return 0

    half = nz // 4
    lax.fori_loop(0, half, solve, 0)

    for peer in others:
        remote(zplanes.at[peer], zplanes.at[peer], z_send.at[0], z_recv.at[peer],
               {"gx": ix, "gy": iy, "gz": peer}).wait_recv()
    packed = nil
    for p in range(PLANES):
        plane = zplanes[0, p]
        for i in range(1, ngz):
            plane = plane + zplanes[i, p]
        ext[p, own, :] = plane
        packed = jnp.where(lax.shift_right_logical(lane, 4) == p, pltpu.roll(plane, 2 * HALO * p + HALO, 1), packed)
    cxsend[...] = packed

    low, high = slice(0, HALO), slice(ny - HALO, ny)
    elow, ehigh = slice(0, HALO), slice(HALO + ny, 2 * HALO + ny)
    coarse = []
    for s, (dy, dx) in enumerate(SIDES):
        rows = low if dy < 0 else high
        into = ehigh if dy < 0 else elow
        if dx == 0:
            src, dst = ext.at[:, slice(rows.start + HALO, rows.stop + HALO)], ext.at[:, into]
        elif dy == 0:
            src, dst = cxsend, cxrecv.at[0 if dx > 0 else 1, own]
        else:
            src, dst = cxsend.at[rows], cxrecv.at[0 if dx > 0 else 1, into]
        coarse.append((exists(dy, dx), exists(-dy, -dx), remote(src, dst, c_send.at[s], c_recv.at[s], at(dy, dx))))
    start(coarse)
    lax.fori_loop(half, nz, solve, 0)
    wait_recv(coarse)

    rows = ny + 2 * HALO
    elane = lax.broadcasted_iota(jnp.int32, (rows, nx), 1)
    efirst, elast = elane == 0, elane == nx - 1
    near = jnp.logical_or(elane < HALO, elane >= nx - HALO)
    beside = jnp.where(lax.rem(elane, 2 * HALO) < HALO, cxrecv[0], cxrecv[1])
    a = [ext[p] for p in range(PLANES)]
    b = [jnp.where(near, pltpu.roll(beside, nx - (2 * HALO * p + HALO), 1), 0.0) for p in range(PLANES)]

    def east(a, b):
        ra, rb = pltpu.roll(a, nx - 1, 1), pltpu.roll(b, nx - 1, 1)
        return jnp.where(elast, rb, ra), jnp.where(elast, ra, rb)

    def west(a, b):
        ra, rb = pltpu.roll(a, 1, 1), pltpu.roll(b, 1, 1)
        return jnp.where(efirst, rb, ra), jnp.where(efirst, ra, rb)

    mid = slice(HALO, HALO + rows)
    wests = west(a[3], b[3])
    terms = []
    for s, planes in enumerate((a, b)):
        there = planes[1] > 0.0
        inv = jnp.where(there, RELAX / jnp.where(there, planes[1], 1.0), 0.0)
        field[s, mid, :] = planes[2]
        south = field[s, HALO - 1:HALO - 1 + rows, :]
        terms.append((planes[0] * inv, planes[2] * inv, south * inv, planes[3] * inv, wests[s] * inv))

    c = [terms[0][0], terms[1][0]]
    for sweep in range(1, SWEEPS):
        e, ws = east(*c), west(*c)
        for s in range(2):
            field[s, mid, :] = c[s]
        nxt = []
        for s in range(2):
            r, tyn, tys, txe, txw = terms[s]
            nxt.append((1.0 - RELAX) * c[s] + r
                       + tyn * field[s, HALO + 1:HALO + 1 + rows, :] + tys * field[s, HALO - 1:HALO - 1 + rows, :]
                       + txe * e[s] + txw * ws[s])
        c = nxt
    e, ws = east(*c), west(*c)
    final[0] = c[0]
    final[1] = e[0]
    final[2] = ws[0]
    wait_send(halos)
    for copy in sums:
        copy.wait_send()
    wait_send(coarse)


def finish_kernel(parts, w, qv, tzs, ty, txp, txm, final, new_hbm, corr_ref, out, out_sem):
    nz, ny, nx = tzs.shape
    own = slice(HALO, HALO + ny)
    cc, ce, cw = (final[k, own, :] for k in range(3))
    cn, cs = final[0, HALO + 1:HALO + 1 + ny, :], final[0, HALO - 1:HALO - 1 + ny, :]
    corr_ref[...] = cc

    def finish(z, _):
        g = (tzs[z] * cc + ty[z, own, :] * cn + ty[z, HALO - 1:HALO + ny - 1, :] * cs
             + txp[z] * ce + txm[z] * cw)
        for r in range(3):
            out[r, z] = w[r, z] + qv[r, z] * g
        return 0

    step = nz // parts
    outs = []
    for part in range(parts):
        lax.fori_loop(part * step, (part + 1) * step, finish, 0)
        chunk = slice(part * step, (part + 1) * step)
        outs.append(pltpu.make_async_copy(out.at[:, chunk], new_hbm.at[:, chunk], out_sem.at[part]))
        outs[-1].start()
    for copy in outs:
        copy.wait()


def per_device(sizes, state, right_side, permeability, pore_volume, facies, storage_table, coupling_table):
    _, nz, ny, nx = state.shape
    sizes = sizes + (nz, ny, nx)
    f32 = jnp.float32
    ngz = sizes[2]
    cells = (nz, ny, nx)
    vmem = lambda *shape: pltpu.VMEM(shape, f32)
    hbm = pl.BlockSpec(memory_space=pltpu.HBM)
    smem = pl.BlockSpec(memory_space=pltpu.SMEM)
    dma = lambda n: pltpu.SemaphoreType.DMA((n,))
    ey = ny + 2 * HALO
    in_vmem = pl.BlockSpec(memory_space=pltpu.VMEM)
    handed = 4 * nx * (9 * nz * ny + nz * ey + 3 * ey)
    limit = 16384 * ((VMEM_BYTES - handed) // 16384)
    middle = pl.pallas_call(
        functools.partial(kernel, sizes),
        out_shape=(vmem(3, *cells), vmem(3, *cells), vmem(*cells), vmem(nz, ey, nx), vmem(*cells), vmem(*cells),
                   vmem(3, ey, nx)),
        in_specs=[smem, smem, smem, hbm, hbm, hbm, hbm],
        out_specs=(in_vmem,) * 7,
        scratch_shapes=[
            vmem(4, nz + 2, ey, nx), vmem(3, *cells),
            pltpu.VMEM(cells, permeability.dtype), pltpu.VMEM(cells, pore_volume.dtype),
            vmem(2, 4 * nz, nx), vmem(2, 4 * nz, nx), vmem(ny, nx), vmem(2, ny, nx),
            vmem(3, *cells), vmem(*cells),
            vmem(ngz, PLANES, ny, nx), vmem(PLANES, ey, nx),
            vmem(ny, nx), vmem(2, ey, nx), vmem(2, ey + 2 * HALO, nx),
            dma(4), dma(6), dma(6), dma(max(ngz - 1, 1)), dma(ngz), dma(8), dma(8),
        ],
        compiler_params=pltpu.CompilerParams(collective_id=0, has_side_effects=True, vmem_limit_bytes=limit),
        name="cpr_apply",
    )(facies, storage_table.transpose(1, 0, 2), coupling_table.transpose(1, 0, 2),
      state, right_side, permeability, pore_volume)
    parts = 4
    return tuple(pl.pallas_call(
        functools.partial(finish_kernel, parts),
        out_shape=(jax.ShapeDtypeStruct(state.shape, f32), jax.ShapeDtypeStruct((ny, nx), f32)),
        in_specs=[in_vmem] * 7,
        out_specs=(hbm, in_vmem),
        scratch_shapes=[vmem(3, *cells), dma(parts)],
        compiler_params=pltpu.CompilerParams(vmem_limit_bytes=16 * 2**20),
        name="cpr_finish",
    )(*middle))


def solution(mesh):
    sizes = (mesh.shape["gx"], mesh.shape["gy"], mesh.shape["gz"])
    return jax.shard_map(
        functools.partial(per_device, sizes),
        mesh=mesh,
        in_specs=(
            P(None, "gz", "gy", "gx"),
            P(None, "gz", "gy", "gx"),
            P("gz", "gy", "gx"),
            P("gz", "gy", "gx"),
            P("gz"),
            P(),
            P(),
        ),
        out_specs=(P(None, "gz", "gy", "gx"), P("gy", "gx")),
        check_vma=False,
    )
```

```python
import functools
import jax
import jax.numpy as jnp
from jax import lax
from jax.experimental import pallas as pl
from jax.experimental.pallas import tpu as pltpu
from jax.sharding import PartitionSpec as P

SWEEPS = 8
RELAX = 0.8
MESH = pl.DeviceIdType.MESH
HALO = 8
VMEM_BYTES = 67043328

PLANES = 4
SIDES = [(-1, 0), (1, 0), (0, -1), (0, 1), (-1, -1), (-1, 1), (1, -1), (1, 1)]


def face(a, b):
    return 2.0 * a * b / (a + b)


def kernel(sizes, facies, mtab, ktab, state_hbm, rhs_hbm, perm_hbm, pore_hbm,
           w, qv, tzs, ty, txp, txm, final,
           u, rhs, permb, poreb, ysend, yrecv, xsend, xrecv, zrecv, yedge, rowk,
           flux, tot, zplanes, ext, cxsend, cxrecv, field,
           in_sem, h_send, h_recv, z_send, z_recv, c_send, c_recv):
    ngx, ngy, ngz, nz, ny, nx = sizes
    ix, iy, iz = lax.axis_index("gx"), lax.axis_index("gy"), lax.axis_index("gz")
    own = slice(HALO, HALO + ny)

    loads = [
        pltpu.make_async_copy(perm_hbm, permb, in_sem.at[0]),
        pltpu.make_async_copy(state_hbm, u.at[0:3, 1:nz + 1, own], in_sem.at[1]),
        pltpu.make_async_copy(pore_hbm, poreb, in_sem.at[2]),
        pltpu.make_async_copy(rhs_hbm, rhs, in_sem.at[3]),
    ]
    for load in loads:
        load.start()

    def exists(dy, dx):
        ok = None
        for d, i, n in ((dy, iy, ngy), (dx, ix, ngx)):
            if d:
                here = (i > 0) if d < 0 else (i < n - 1)
                ok = here if ok is None else jnp.logical_and(ok, here)
        return ok

    def at(dy, dx):
        return {"gx": ix + dx, "gy": iy + dy, "gz": iz}

    barrier = pltpu.get_barrier_semaphore()
    for side in SIDES:
        @pl.when(exists(*side))
        def _(side=side):
            pl.semaphore_signal(barrier, inc=1, device_id=at(*side), device_id_type=MESH)
    for d in range(1, ngz):
        pl.semaphore_signal(barrier, inc=1, device_id={"gx": ix, "gy": iy, "gz": lax.rem(iz + d, ngz)},
                            device_id_type=MESH)

    lane = lax.broadcasted_iota(jnp.int32, (ny, nx), 1)

    def zero(ref):
        ref[...] = jnp.zeros(ref.shape, ref.dtype)

    for cond, refs in (
        (iz == 0, [zrecv.at[0]]),
        (iz == ngz - 1, [zrecv.at[1]]),
        (iy == 0, [yrecv.at[0], ext.at[:, 0:HALO]]),
        (iy == ngy - 1, [yrecv.at[1], ext.at[:, HALO + ny:]]),
        (ix == 0, [xrecv.at[0], cxrecv.at[0, own]]),
        (ix == ngx - 1, [xrecv.at[1], cxrecv.at[1, own]]),
        (jnp.logical_or(iy == 0, ix == 0), [cxrecv.at[0, 0:HALO]]),
        (jnp.logical_or(iy == 0, ix == ngx - 1), [cxrecv.at[1, 0:HALO]]),
        (jnp.logical_or(iy == ngy - 1, ix == 0), [cxrecv.at[0, HALO + ny:]]),
        (jnp.logical_or(iy == ngy - 1, ix == ngx - 1), [cxrecv.at[1, HALO + ny:]]),
    ):
        @pl.when(cond)
        def _(refs=refs):
            for ref in refs:
                zero(ref)
    zero(field)
    zero(u.at[:, nz + 1, own])
    zero(u.at[:, 0, own])

    loads[0].wait()

    def loop(begin, end, body, carry, unroll):
        def several(i, carry):
            for k in range(unroll):
                carry = body(begin + i * unroll + k, carry)
            return carry
        return lax.fori_loop(0, (end - begin) // unroll, several, carry)

    def coefficient(table, z, r, c):
        return table[r, facies[z], c]

    def widen(z, _):
        u[3, z + 1, own, :] = permb[z].astype(jnp.float32)
        for k in range(4):
            u[k, z + 1, 0:HALO, :] = jnp.zeros((HALO, nx), jnp.float32)
            u[k, z + 1, HALO + ny:, :] = jnp.zeros((HALO, nx), jnp.float32)
            rowk[pl.ds(k * nz + z, 1), :] = jnp.full((1, nx), coefficient(ktab, z, 0, k % 3), jnp.float32)
        return 0

    loop(0, nz, widen, 0, 2)
    loads[1].wait()

    def pack_rows(z, _):
        for k in range(4):
            j = k * nz + z
            ysend[0, pl.ds(j, 1), :] = u[k, z + 1, HALO:HALO + 1, :]
            ysend[1, pl.ds(j, 1), :] = u[k, z + 1, HALO + ny - 1:HALO + ny, :]
        return 0

    loop(0, nz, pack_rows, 0, 4)

    count = sum(exists(*side).astype(jnp.int32) for side in SIDES) + (ngz - 1)
    pl.semaphore_wait(barrier, count)

    def remote(src, dst, send, recv, device):
        return pltpu.make_async_remote_copy(src_ref=src, dst_ref=dst, send_sem=send, recv_sem=recv,
                                            device_id=device, device_id_type=MESH)

    def z_device(d):
        return {"gx": ix, "gy": iy, "gz": iz + d}

    halos = [
        (iz < ngz - 1, iz > 0, remote(u.at[:, nz, own], zrecv.at[0], h_send.at[0], h_recv.at[0], z_device(1))),
        (iz > 0, iz < ngz - 1, remote(u.at[:, 1, own], zrecv.at[1], h_send.at[1], h_recv.at[1], z_device(-1))),
        (exists(1, 0), exists(-1, 0), remote(ysend.at[1], yrecv.at[0], h_send.at[2], h_recv.at[2], at(1, 0))),
        (exists(-1, 0), exists(1, 0), remote(ysend.at[0], yrecv.at[1], h_send.at[3], h_recv.at[3], at(-1, 0))),
        (exists(0, 1), exists(0, -1), remote(xsend, xrecv.at[0], h_send.at[4], h_recv.at[4], at(0, 1))),
        (exists(0, -1), exists(0, 1), remote(xsend, xrecv.at[1], h_send.at[5], h_recv.at[5], at(0, -1))),
    ]

    def start(copies):
        for sends, _, copy in copies:
            @pl.when(sends)
            def _(copy=copy):
                copy.start()

    def wait_recv(copies):
        for _, gets, copy in copies:
            @pl.when(gets)
            def _(copy=copy):
                copy.wait_recv()

    def wait_send(copies):
        for sends, _, copy in copies:
            @pl.when(sends)
            def _(copy=copy):
                copy.wait_send()

    start(halos[:4])

    lane_row = lane[0:1]

    def pack_columns(z, carry):
        packed, lanek = carry
        for k in range(4):
            j = k * nz + z
            packed = jnp.where(lax.shift_right_logical(lane, 1) == j,
                               pltpu.roll(u[k, z + 1, own, :], lax.rem(2 * j + 1, nx), 1), packed)
            lanek = jnp.where(lax.shift_right_logical(lane_row, 1) == j, coefficient(ktab, z, 0, k % 3), lanek)
        return packed, lanek

    nil = jnp.zeros((ny, nx), jnp.float32)
    packed, lanek = loop(0, nz, pack_columns, (nil, jnp.zeros((1, nx), jnp.float32)), 4)
    xsend[...] = packed
    start(halos[4:])
    loads[2].wait()
    loads[3].wait()

    first, last = lane == 0, lane == nx - 1

    def assemble(z, carry):
        tzm, s_rhs, s_diag, s_ty, s_tx = carry
        q = u[3, z + 1, own, :]
        tzp = face(q, u[3, z + 2, own, :])
        typ = face(q, u[3, z + 1, HALO + 1:HALO + ny + 1, :])
        ty[z, own, :] = typ
        ty[z, 0:HALO, :] = jnp.zeros((HALO, nx), jnp.float32)
        tym = ty[z, HALO - 1:HALO + ny - 1, :]
        xp = jnp.where(last, 0.0, face(q, pltpu.roll(q, nx - 1, 1)))
        xm = pltpu.roll(xp, 1, 1)
        txp[z] = xp
        txm[z] = xm
        tz = tzp + tzm
        areal = typ + tym + xp + xm
        tzs[z] = tz
        tot[z] = tz + areal
        v = poreb[z].astype(jnp.float32)
        local, moved = 0.0, 0.0
        for k in range(3):
            c = u[k, z + 1, own, :]
            f = (tzp * (c - u[k, z + 2, own, :]) + tzm * (c - u[k, z, own, :])
                 + typ * (c - u[k, z + 1, HALO + 1:HALO + ny + 1, :])
                 + tym * (c - u[k, z + 1, HALO - 1:HALO + ny - 1, :])
                 + xp * (c - pltpu.roll(c, nx - 1, 1)) + xm * (c - pltpu.roll(c, 1, 1)))
            flux[k, z] = f
            local = local + coefficient(mtab, z, 0, k) * c
            moved = moved + coefficient(ktab, z, 0, k) * f
        res = rhs[0, z] - (v * local + moved)
        k00 = coefficient(ktab, z, 0, 0)
        return (tzp, s_rhs + res, s_diag + (v * coefficient(mtab, z, 0, 0) + k00 * areal),
                s_ty + k00 * typ, s_tx + k00 * xp)

    _, s_rhs, s_diag, s_ty, s_tx = loop(0, nz, assemble, (nil,) * 5, 2)
    wait_recv(halos)

    for side, z in ((0, 0), (1, nz - 1)):
        t = face(u[3, z + 1, own, :], zrecv[side, 3])
        for k in range(3):
            f = t * (u[k, z + 1, own, :] - zrecv[side, k])
            flux[k, z] = flux[k, z] + f
            s_rhs = s_rhs - coefficient(ktab, z, 0, k) * f
        tzs[z] = tzs[z] + t
        tot[z] = tot[z] + t

    row = lax.broadcasted_iota(jnp.int32, (ny, nx), 0)
    for side, at_row in ((0, 0), (1, ny - 1)):
        t = face(ysend[side, 3 * nz:, :], yrecv[side, 3 * nz:, :])
        f = [t * (ysend[side, k * nz:(k + 1) * nz, :] - yrecv[side, k * nz:(k + 1) * nz, :]) for k in range(3)]
        for k, x in enumerate(f + [t]):
            yedge[side, k * nz:(k + 1) * nz, :] = x
        moved = sum(rowk[k * nz:(k + 1) * nz, :] * f[k] for k in range(3))
        moved = jnp.sum(moved, axis=0, keepdims=True)
        weight = jnp.sum(rowk[3 * nz:, :] * t, axis=0, keepdims=True)
        here = row == at_row
        s_rhs = s_rhs - jnp.where(here, moved, 0.0)
        s_diag = s_diag + jnp.where(here, weight, 0.0)
        if side:
            s_ty = s_ty + jnp.where(here, weight, 0.0)

    even = lax.rem(lane, 2) == 0
    weights_at = jnp.logical_and(even, lane >= 6 * nz)
    fluxes_at = jnp.logical_and(even, lane < 6 * nz)
    edges = []
    for side, edge in ((0, first), (1, last)):
        if side:
            here, there = xsend[...], pltpu.roll(xrecv[1], nx - 1, 1)
        else:
            here, there = pltpu.roll(xsend[...], nx - 1, 1), xrecv[0]
        t = jnp.where(weights_at, face(jnp.where(weights_at, here, 1.0), jnp.where(weights_at, there, 1.0)), 0.0)
        every = sum(pltpu.roll(t, nx - 2 * (3 - k) * nz, 1) for k in range(3))
        f = jnp.where(fluxes_at, every * (here - there), 0.0)
        moved = jnp.sum(f * lanek, axis=1, keepdims=True)
        weight = jnp.sum(t * lanek, axis=1, keepdims=True)
        s_rhs = s_rhs - jnp.where(edge, moved, 0.0)
        s_diag = s_diag + jnp.where(edge, weight, 0.0)
        if side:
            s_tx = s_tx + jnp.where(edge, weight, 0.0)
        edges.append(f + t)
    border = jnp.where(even, edges[0], pltpu.roll(edges[1], nx - 1, 1))

    for p, plane in enumerate((s_rhs, s_diag, s_ty, s_tx)):
        zplanes[iz, p] = plane

    others = [lax.rem(iz + d, ngz) for d in range(1, ngz)]
    sums = [remote(zplanes.at[iz], zplanes.at[iz], z_send.at[d], z_recv.at[iz], {"gx": ix, "gy": iy, "gz": peer})
            for d, peer in enumerate(others)]
    for copy in sums:
        copy.start()

    outer = jnp.logical_or(first, last)

    def solve(z, _):
        v = poreb[z].astype(jnp.float32)
        for side, at_row in ((0, 0), (1, ny - 1)):
            here = slice(at_row, at_row + 1)
            for k in range(3):
                flux[k, z, here, :] = flux[k, z, here, :] + yedge[side, pl.ds(k * nz + z, 1), :]
            t = yedge[side, pl.ds(3 * nz + z, 1), :]
            tot[z, here, :] = tot[z, here, :] + t
            at_face = HALO - 1 + side * ny
            ty[z, at_face:at_face + 1, :] = t

        def beside(k):
            shifted = pltpu.roll(border, lax.rem(2 * nx - 2 * (k * nz + z), nx), 1)
            return jnp.where(outer, shifted, 0.0)

        t = beside(3)
        txp[z] = txp[z] + jnp.where(last, t, 0.0)
        txm[z] = txm[z] + jnp.where(first, t, 0.0)
        total = tot[z] + t
        m = [[coefficient(mtab, z, r, c) for c in range(3)] for r in range(3)]
        kk = [[coefficient(ktab, z, r, c) for c in range(3)] for r in range(3)]
        e = [[v * m[r][c] + total * kk[r][c] for c in range(3)] for r in range(3)]

        def cofactor(r, c):
            return (e[(r + 1) % 3][(c + 1) % 3] * e[(r + 2) % 3][(c + 2) % 3]
                    - e[(r + 1) % 3][(c + 2) % 3] * e[(r + 2) % 3][(c + 1) % 3])

        cells = [u[k, z + 1, own, :] for k in range(3)]
        f = [flux[k, z] + beside(k) for k in range(3)]
        res = []
        for r in range(3):
            res.append(rhs[r, z] - (v * (m[r][0] * cells[0] + m[r][1] * cells[1] + m[r][2] * cells[2])
                                    + (kk[r][0] * f[0] + kk[r][1] * f[1] + kk[r][2] * f[2])))
        fac = [[cofactor(r, c) for c in range(3)] for r in range(3)]
        inv = 1.0 / (e[0][0] * fac[0][0] + e[0][1] * fac[0][1] + e[0][2] * fac[0][2])
        for r in range(3):
            w[r, z] = cells[r] + (fac[0][r] * res[0] + fac[1][r] * res[1] + fac[2][r] * res[2]) * inv
            qv[r, z] = (fac[0][r] * kk[0][0] + fac[1][r] * kk[1][0] + fac[2][r] * kk[2][0]) * inv
        return 0

    half = nz // 4
    loop(0, half, solve, 0, 2)

    for peer in others:
        remote(zplanes.at[peer], zplanes.at[peer], z_send.at[0], z_recv.at[peer],
               {"gx": ix, "gy": iy, "gz": peer}).wait_recv()
    packed = nil
    for p in range(PLANES):
        plane = zplanes[0, p]
        for i in range(1, ngz):
            plane = plane + zplanes[i, p]
        ext[p, own, :] = plane
        packed = jnp.where(lax.shift_right_logical(lane, 4) == p, pltpu.roll(plane, 2 * HALO * p + HALO, 1), packed)
    cxsend[...] = packed

    low, high = slice(0, HALO), slice(ny - HALO, ny)
    elow, ehigh = slice(0, HALO), slice(HALO + ny, 2 * HALO + ny)
    coarse = []
    for s, (dy, dx) in enumerate(SIDES):
        rows = low if dy < 0 else high
        into = ehigh if dy < 0 else elow
        if dx == 0:
            src, dst = ext.at[:, slice(rows.start + HALO, rows.stop + HALO)], ext.at[:, into]
        elif dy == 0:
            src, dst = cxsend, cxrecv.at[0 if dx > 0 else 1, own]
        else:
            src, dst = cxsend.at[rows], cxrecv.at[0 if dx > 0 else 1, into]
        coarse.append((exists(dy, dx), exists(-dy, -dx), remote(src, dst, c_send.at[s], c_recv.at[s], at(dy, dx))))
    start(coarse)
    loop(half, nz, solve, 0, 2)
    wait_recv(coarse)

    rows = ny + 2 * HALO
    elane = lax.broadcasted_iota(jnp.int32, (rows, nx), 1)
    efirst, elast = elane == 0, elane == nx - 1
    near = jnp.logical_or(elane < HALO, elane >= nx - HALO)
    beside = jnp.where(lax.rem(elane, 2 * HALO) < HALO, cxrecv[0], cxrecv[1])
    a = [ext[p] for p in range(PLANES)]
    b = [jnp.where(near, pltpu.roll(beside, nx - (2 * HALO * p + HALO), 1), 0.0) for p in range(PLANES)]

    def east(a, b):
        ra, rb = pltpu.roll(a, nx - 1, 1), pltpu.roll(b, nx - 1, 1)
        return jnp.where(elast, rb, ra), jnp.where(elast, ra, rb)

    def west(a, b):
        ra, rb = pltpu.roll(a, 1, 1), pltpu.roll(b, 1, 1)
        return jnp.where(efirst, rb, ra), jnp.where(efirst, ra, rb)

    mid = slice(HALO, HALO + rows)
    wests = west(a[3], b[3])
    terms = []
    for s, planes in enumerate((a, b)):
        there = planes[1] > 0.0
        inv = jnp.where(there, RELAX / jnp.where(there, planes[1], 1.0), 0.0)
        field[s, mid, :] = planes[2]
        south = field[s, HALO - 1:HALO - 1 + rows, :]
        terms.append((planes[0] * inv, planes[2] * inv, south * inv, planes[3] * inv, wests[s] * inv))

    c = [terms[0][0], terms[1][0]]
    for sweep in range(1, SWEEPS):
        e, ws = east(*c), west(*c)
        for s in range(2):
            field[s, mid, :] = c[s]
        nxt = []
        for s in range(2):
            r, tyn, tys, txe, txw = terms[s]
            nxt.append((1.0 - RELAX) * c[s] + r
                       + tyn * field[s, HALO + 1:HALO + 1 + rows, :] + tys * field[s, HALO - 1:HALO - 1 + rows, :]
                       + txe * e[s] + txw * ws[s])
        c = nxt
    e, ws = east(*c), west(*c)
    final[0] = c[0]
    final[1] = e[0]
    final[2] = ws[0]
    wait_send(halos)
    for copy in sums:
        copy.wait_send()
    wait_send(coarse)


def finish_kernel(parts, w, qv, tzs, ty, txp, txm, final, new_hbm, corr_ref, out, out_sem):
    nz, ny, nx = tzs.shape
    own = slice(HALO, HALO + ny)
    cc, ce, cw = (final[k, own, :] for k in range(3))
    cn, cs = final[0, HALO + 1:HALO + 1 + ny, :], final[0, HALO - 1:HALO - 1 + ny, :]
    corr_ref[...] = cc

    def finish(z, _):
        g = (tzs[z] * cc + ty[z, own, :] * cn + ty[z, HALO - 1:HALO + ny - 1, :] * cs
             + txp[z] * ce + txm[z] * cw)
        for r in range(3):
            out[r, z] = w[r, z] + qv[r, z] * g
        return 0

    step = nz // parts
    outs = []
    for part in range(parts):
        lax.fori_loop(part * step, (part + 1) * step, finish, 0)
        chunk = slice(part * step, (part + 1) * step)
        outs.append(pltpu.make_async_copy(out.at[:, chunk], new_hbm.at[:, chunk], out_sem.at[part]))
        outs[-1].start()
    for copy in outs:
        copy.wait()


def per_device(sizes, state, right_side, permeability, pore_volume, facies, storage_table, coupling_table):
    _, nz, ny, nx = state.shape
    sizes = sizes + (nz, ny, nx)
    f32 = jnp.float32
    ngz = sizes[2]
    cells = (nz, ny, nx)
    vmem = lambda *shape: pltpu.VMEM(shape, f32)
    hbm = pl.BlockSpec(memory_space=pltpu.HBM)
    smem = pl.BlockSpec(memory_space=pltpu.SMEM)
    dma = lambda n: pltpu.SemaphoreType.DMA((n,))
    ey = ny + 2 * HALO
    in_vmem = pl.BlockSpec(memory_space=pltpu.VMEM)
    handed = 4 * nx * (9 * nz * ny + nz * ey + 3 * ey)
    limit = 16384 * ((VMEM_BYTES - handed) // 16384)
    middle = pl.pallas_call(
        functools.partial(kernel, sizes),
        out_shape=(vmem(3, *cells), vmem(3, *cells), vmem(*cells), vmem(nz, ey, nx), vmem(*cells), vmem(*cells),
                   vmem(3, ey, nx)),
        in_specs=[smem, smem, smem, hbm, hbm, hbm, hbm],
        out_specs=(in_vmem,) * 7,
        scratch_shapes=[
            vmem(4, nz + 2, ey, nx), vmem(3, *cells),
            pltpu.VMEM(cells, permeability.dtype), pltpu.VMEM(cells, pore_volume.dtype),
            vmem(2, 4 * nz, nx), vmem(2, 4 * nz, nx), vmem(ny, nx), vmem(2, ny, nx),
            vmem(2, 4, ny, nx), vmem(2, 4 * nz, nx), vmem(4 * nz, nx),
            vmem(3, *cells), vmem(*cells),
            vmem(ngz, PLANES, ny, nx), vmem(PLANES, ey, nx),
            vmem(ny, nx), vmem(2, ey, nx), vmem(2, ey + 2 * HALO, nx),
            dma(4), dma(6), dma(6), dma(max(ngz - 1, 1)), dma(ngz), dma(8), dma(8),
        ],
        compiler_params=pltpu.CompilerParams(collective_id=0, has_side_effects=True, vmem_limit_bytes=limit),
        name="cpr_apply",
    )(facies, storage_table.transpose(1, 0, 2), coupling_table.transpose(1, 0, 2),
      state, right_side, permeability, pore_volume)
    parts = 4
    return tuple(pl.pallas_call(
        functools.partial(finish_kernel, parts),
        out_shape=(jax.ShapeDtypeStruct(state.shape, f32), jax.ShapeDtypeStruct((ny, nx), f32)),
        in_specs=[in_vmem] * 7,
        out_specs=(hbm, in_vmem),
        scratch_shapes=[vmem(3, *cells), dma(parts)],
        compiler_params=pltpu.CompilerParams(vmem_limit_bytes=16 * 2**20),
        name="cpr_finish",
    )(*middle))


def solution(mesh):
    sizes = (mesh.shape["gx"], mesh.shape["gy"], mesh.shape["gz"])
    return jax.shard_map(
        functools.partial(per_device, sizes),
        mesh=mesh,
        in_specs=(
            P(None, "gz", "gy", "gx"),
            P(None, "gz", "gy", "gx"),
            P("gz", "gy", "gx"),
            P("gz", "gy", "gx"),
            P("gz"),
            P(),
            P(),
        ),
        out_specs=(P(None, "gz", "gy", "gx"), P("gy", "gx")),
        check_vma=False,
    )
```

```python
import functools
import jax
import jax.numpy as jnp
from jax import lax
from jax.experimental import pallas as pl
from jax.experimental.pallas import tpu as pltpu
from jax.sharding import PartitionSpec as P

SWEEPS = 8
RELAX = 0.8
MESH = pl.DeviceIdType.MESH
HALO = 8
VMEM_BYTES = 67043328

PLANES = 4
SIDES = [(-1, 0), (1, 0), (0, -1), (0, 1), (-1, -1), (-1, 1), (1, -1), (1, 1)]


def face(a, b):
    return 2.0 * a * b / (a + b)


def kernel(sizes, facies_hbm, mtab_hbm, ktab_hbm, state_hbm, rhs_hbm, perm_hbm, pore_hbm,
           w, qv, tzs, ty, txp, txm, final,
           u, rhs, permb, poreb, ysend, yrecv, xsend, xrecv, zrecv, yedge, rowk,
           flux, tot, zplanes, ext, cxsend, cxrecv, field,
           facies, mtab, ktab, near_sem, in_sem, h_send, h_recv, z_send, z_recv, c_send, c_recv):
    ngx, ngy, ngz, nz, ny, nx = sizes
    ix, iy, iz = lax.axis_index("gx"), lax.axis_index("gy"), lax.axis_index("gz")
    own = slice(HALO, HALO + ny)

    def exists(dy, dx):
        ok = None
        for d, i, n in ((dy, iy, ngy), (dx, ix, ngx)):
            if d:
                here = (i > 0) if d < 0 else (i < n - 1)
                ok = here if ok is None else jnp.logical_and(ok, here)
        return ok

    def at(dy, dx):
        return {"gx": ix + dx, "gy": iy + dy, "gz": iz}

    barrier = pltpu.get_barrier_semaphore()
    for side in SIDES[:4]:
        @pl.when(exists(*side))
        def _(side=side):
            pl.semaphore_signal(barrier, inc=1, device_id=at(*side), device_id_type=MESH)
    for d in range(1, ngz):
        pl.semaphore_signal(barrier, inc=1, device_id={"gx": ix, "gy": iy, "gz": lax.rem(iz + d, ngz)},
                            device_id_type=MESH)

    loads = [
        pltpu.make_async_copy(perm_hbm, permb, in_sem.at[0]),
        pltpu.make_async_copy(state_hbm, u.at[0:3, 1:nz + 1, own], in_sem.at[1]),
        pltpu.make_async_copy(pore_hbm, poreb, in_sem.at[2]),
        pltpu.make_async_copy(rhs_hbm, rhs, in_sem.at[3]),
        pltpu.make_async_copy(facies_hbm, facies, in_sem.at[4]),
        pltpu.make_async_copy(mtab_hbm, mtab, in_sem.at[5]),
        pltpu.make_async_copy(ktab_hbm, ktab, in_sem.at[6]),
    ]
    for load in loads:
        load.start()

    lane = lax.broadcasted_iota(jnp.int32, (ny, nx), 1)

    def zero(ref):
        ref[...] = jnp.zeros(ref.shape, ref.dtype)

    for cond, refs in (
        (iz == 0, [zrecv.at[0]]),
        (iz == ngz - 1, [zrecv.at[1]]),
        (iy == 0, [yrecv.at[0], ext.at[:, 0:HALO]]),
        (iy == ngy - 1, [yrecv.at[1], ext.at[:, HALO + ny:]]),
        (ix == 0, [xrecv.at[0], cxrecv.at[0, own]]),
        (ix == ngx - 1, [xrecv.at[1], cxrecv.at[1, own]]),
        (jnp.logical_or(iy == 0, ix == 0), [cxrecv.at[0, 0:HALO]]),
        (jnp.logical_or(iy == 0, ix == ngx - 1), [cxrecv.at[1, 0:HALO]]),
        (jnp.logical_or(iy == ngy - 1, ix == 0), [cxrecv.at[0, HALO + ny:]]),
        (jnp.logical_or(iy == ngy - 1, ix == ngx - 1), [cxrecv.at[1, HALO + ny:]]),
    ):
        @pl.when(cond)
        def _(refs=refs):
            for ref in refs:
                zero(ref)
    zero(field)
    zero(u.at[:, nz + 1, own])
    zero(u.at[:, 0, own])

    loads[0].wait()
    for load in loads[4:]:
        load.wait()

    def loop(begin, end, body, carry, unroll):
        def several(i, carry):
            for k in range(unroll):
                carry = body(begin + i * unroll + k, carry)
            return carry
        return lax.fori_loop(0, (end - begin) // unroll, several, carry)

    def coefficient(table, z, r, c):
        return table[r, facies[z], c]

    def widen(z, _):
        u[3, z + 1, own, :] = permb[z].astype(jnp.float32)
        for k in range(4):
            u[k, z + 1, 0:HALO, :] = jnp.zeros((HALO, nx), jnp.float32)
            u[k, z + 1, HALO + ny:, :] = jnp.zeros((HALO, nx), jnp.float32)
            rowk[pl.ds(k * nz + z, 1), :] = jnp.full((1, nx), coefficient(ktab, z, 0, k % 3), jnp.float32)
        return 0

    loop(0, nz, widen, 0, 2)
    loads[1].wait()

    def pack_rows(z, _):
        for k in range(4):
            j = k * nz + z
            ysend[0, pl.ds(j, 1), :] = u[k, z + 1, HALO:HALO + 1, :]
            ysend[1, pl.ds(j, 1), :] = u[k, z + 1, HALO + ny - 1:HALO + ny, :]
        return 0

    loop(0, nz, pack_rows, 0, 4)

    count = sum(exists(*side).astype(jnp.int32) for side in SIDES[:4])
    pl.semaphore_wait(barrier, count + (ngz - 1))
    for side in SIDES[:4]:
        @pl.when(exists(*side))
        def _(side=side):
            pl.semaphore_signal(near_sem, inc=1, device_id=at(*side), device_id_type=MESH)

    def remote(src, dst, send, recv, device):
        return pltpu.make_async_remote_copy(src_ref=src, dst_ref=dst, send_sem=send, recv_sem=recv,
                                            device_id=device, device_id_type=MESH)

    def z_device(d):
        return {"gx": ix, "gy": iy, "gz": iz + d}

    halos = [
        (iz < ngz - 1, iz > 0, remote(u.at[:, nz, own], zrecv.at[0], h_send.at[0], h_recv.at[0], z_device(1))),
        (iz > 0, iz < ngz - 1, remote(u.at[:, 1, own], zrecv.at[1], h_send.at[1], h_recv.at[1], z_device(-1))),
        (exists(1, 0), exists(-1, 0), remote(ysend.at[1], yrecv.at[0], h_send.at[2], h_recv.at[2], at(1, 0))),
        (exists(-1, 0), exists(1, 0), remote(ysend.at[0], yrecv.at[1], h_send.at[3], h_recv.at[3], at(-1, 0))),
        (exists(0, 1), exists(0, -1), remote(xsend, xrecv.at[0], h_send.at[4], h_recv.at[4], at(0, 1))),
        (exists(0, -1), exists(0, 1), remote(xsend, xrecv.at[1], h_send.at[5], h_recv.at[5], at(0, -1))),
    ]

    def start(copies):
        for sends, _, copy in copies:
            @pl.when(sends)
            def _(copy=copy):
                copy.start()

    def wait_recv(copies):
        for _, gets, copy in copies:
            @pl.when(gets)
            def _(copy=copy):
                copy.wait_recv()

    def wait_send(copies):
        for sends, _, copy in copies:
            @pl.when(sends)
            def _(copy=copy):
                copy.wait_send()

    start(halos[:4])

    lane_row = lane[0:1]

    def pack_columns(z, carry):
        packed, lanek = carry
        for k in range(4):
            j = k * nz + z
            packed = jnp.where(lax.shift_right_logical(lane, 1) == j,
                               pltpu.roll(u[k, z + 1, own, :], lax.rem(2 * j + 1, nx), 1), packed)
            lanek = jnp.where(lax.shift_right_logical(lane_row, 1) == j, coefficient(ktab, z, 0, k % 3), lanek)
        return packed, lanek

    nil = jnp.zeros((ny, nx), jnp.float32)
    packed, lanek = loop(0, nz, pack_columns, (nil, jnp.zeros((1, nx), jnp.float32)), 4)
    xsend[...] = packed
    start(halos[4:])
    loads[2].wait()
    loads[3].wait()

    first, last = lane == 0, lane == nx - 1

    def assemble(z, carry):
        tzm, s_rhs, s_diag, s_ty, s_tx = carry
        q = u[3, z + 1, own, :]
        tzp = face(q, u[3, z + 2, own, :])
        typ = face(q, u[3, z + 1, HALO + 1:HALO + ny + 1, :])
        ty[z, own, :] = typ
        ty[z, 0:HALO, :] = jnp.zeros((HALO, nx), jnp.float32)
        tym = ty[z, HALO - 1:HALO + ny - 1, :]
        xp = jnp.where(last, 0.0, face(q, pltpu.roll(q, nx - 1, 1)))
        xm = pltpu.roll(xp, 1, 1)
        txp[z] = xp
        txm[z] = xm
        tz = tzp + tzm
        areal = typ + tym + xp + xm
        tzs[z] = tz
        tot[z] = tz + areal
        v = poreb[z].astype(jnp.float32)
        local, moved = 0.0, 0.0
        for k in range(3):
            c = u[k, z + 1, own, :]
            f = (tzp * (c - u[k, z + 2, own, :]) + tzm * (c - u[k, z, own, :])
                 + typ * (c - u[k, z + 1, HALO + 1:HALO + ny + 1, :])
                 + tym * (c - u[k, z + 1, HALO - 1:HALO + ny - 1, :])
                 + xp * (c - pltpu.roll(c, nx - 1, 1)) + xm * (c - pltpu.roll(c, 1, 1)))
            flux[k, z] = f
            local = local + coefficient(mtab, z, 0, k) * c
            moved = moved + coefficient(ktab, z, 0, k) * f
        res = rhs[0, z] - (v * local + moved)
        k00 = coefficient(ktab, z, 0, 0)
        return (tzp, s_rhs + res, s_diag + (v * coefficient(mtab, z, 0, 0) + k00 * areal),
                s_ty + k00 * typ, s_tx + k00 * xp)

    _, s_rhs, s_diag, s_ty, s_tx = loop(0, nz, assemble, (nil,) * 5, 2)
    wait_recv(halos)

    for side, z in ((0, 0), (1, nz - 1)):
        t = face(u[3, z + 1, own, :], zrecv[side, 3])
        for k in range(3):
            f = t * (u[k, z + 1, own, :] - zrecv[side, k])
            flux[k, z] = flux[k, z] + f
            s_rhs = s_rhs - coefficient(ktab, z, 0, k) * f
        tzs[z] = tzs[z] + t
        tot[z] = tot[z] + t

    row = lax.broadcasted_iota(jnp.int32, (ny, nx), 0)
    for side, at_row in ((0, 0), (1, ny - 1)):
        t = face(ysend[side, 3 * nz:, :], yrecv[side, 3 * nz:, :])
        f = [t * (ysend[side, k * nz:(k + 1) * nz, :] - yrecv[side, k * nz:(k + 1) * nz, :]) for k in range(3)]
        for k, x in enumerate(f + [t]):
            yedge[side, k * nz:(k + 1) * nz, :] = x
        moved = sum(rowk[k * nz:(k + 1) * nz, :] * f[k] for k in range(3))
        moved = jnp.sum(moved, axis=0, keepdims=True)
        weight = jnp.sum(rowk[3 * nz:, :] * t, axis=0, keepdims=True)
        here = row == at_row
        s_rhs = s_rhs - jnp.where(here, moved, 0.0)
        s_diag = s_diag + jnp.where(here, weight, 0.0)
        if side:
            s_ty = s_ty + jnp.where(here, weight, 0.0)

    even = lax.rem(lane, 2) == 0
    weights_at = jnp.logical_and(even, lane >= 6 * nz)
    fluxes_at = jnp.logical_and(even, lane < 6 * nz)
    edges = []
    for side, edge in ((0, first), (1, last)):
        if side:
            here, there = xsend[...], pltpu.roll(xrecv[1], nx - 1, 1)
        else:
            here, there = pltpu.roll(xsend[...], nx - 1, 1), xrecv[0]
        t = jnp.where(weights_at, face(jnp.where(weights_at, here, 1.0), jnp.where(weights_at, there, 1.0)), 0.0)
        every = sum(pltpu.roll(t, nx - 2 * (3 - k) * nz, 1) for k in range(3))
        f = jnp.where(fluxes_at, every * (here - there), 0.0)
        moved = jnp.sum(f * lanek, axis=1, keepdims=True)
        weight = jnp.sum(t * lanek, axis=1, keepdims=True)
        s_rhs = s_rhs - jnp.where(edge, moved, 0.0)
        s_diag = s_diag + jnp.where(edge, weight, 0.0)
        if side:
            s_tx = s_tx + jnp.where(edge, weight, 0.0)
        edges.append(f + t)
    border = jnp.where(even, edges[0], pltpu.roll(edges[1], nx - 1, 1))

    for p, plane in enumerate((s_rhs, s_diag, s_ty, s_tx)):
        zplanes[iz, p] = plane

    others = [lax.rem(iz + d, ngz) for d in range(1, ngz)]
    sums = [remote(zplanes.at[iz], zplanes.at[iz], z_send.at[d], z_recv.at[iz], {"gx": ix, "gy": iy, "gz": peer})
            for d, peer in enumerate(others)]
    for copy in sums:
        copy.start()

    outer = jnp.logical_or(first, last)

    def solve(z, _):
        v = poreb[z].astype(jnp.float32)
        for side, at_row in ((0, 0), (1, ny - 1)):
            here = slice(at_row, at_row + 1)
            for k in range(3):
                flux[k, z, here, :] = flux[k, z, here, :] + yedge[side, pl.ds(k * nz + z, 1), :]
            t = yedge[side, pl.ds(3 * nz + z, 1), :]
            tot[z, here, :] = tot[z, here, :] + t
            at_face = HALO - 1 + side * ny
            ty[z, at_face:at_face + 1, :] = t

        def beside(k):
            shifted = pltpu.roll(border, lax.rem(2 * nx - 2 * (k * nz + z), nx), 1)
            return jnp.where(outer, shifted, 0.0)

        t = beside(3)
        txp[z] = txp[z] + jnp.where(last, t, 0.0)
        txm[z] = txm[z] + jnp.where(first, t, 0.0)
        total = tot[z] + t
        m = [[coefficient(mtab, z, r, c) for c in range(3)] for r in range(3)]
        kk = [[coefficient(ktab, z, r, c) for c in range(3)] for r in range(3)]
        e = [[v * m[r][c] + total * kk[r][c] for c in range(3)] for r in range(3)]

        def cofactor(r, c):
            return (e[(r + 1) % 3][(c + 1) % 3] * e[(r + 2) % 3][(c + 2) % 3]
                    - e[(r + 1) % 3][(c + 2) % 3] * e[(r + 2) % 3][(c + 1) % 3])

        cells = [u[k, z + 1, own, :] for k in range(3)]
        f = [flux[k, z] + beside(k) for k in range(3)]
        res = []
        for r in range(3):
            res.append(rhs[r, z] - (v * (m[r][0] * cells[0] + m[r][1] * cells[1] + m[r][2] * cells[2])
                                    + (kk[r][0] * f[0] + kk[r][1] * f[1] + kk[r][2] * f[2])))
        fac = [[cofactor(r, c) for c in range(3)] for r in range(3)]
        inv = 1.0 / (e[0][0] * fac[0][0] + e[0][1] * fac[0][1] + e[0][2] * fac[0][2])
        for r in range(3):
            w[r, z] = cells[r] + (fac[0][r] * res[0] + fac[1][r] * res[1] + fac[2][r] * res[2]) * inv
            qv[r, z] = (fac[0][r] * kk[0][0] + fac[1][r] * kk[1][0] + fac[2][r] * kk[2][0]) * inv
        return 0

    half = nz // 4
    loop(0, half, solve, 0, 2)

    for peer in others:
        remote(zplanes.at[peer], zplanes.at[peer], z_send.at[0], z_recv.at[peer],
               {"gx": ix, "gy": iy, "gz": peer}).wait_recv()
    packed = nil
    for p in range(PLANES):
        plane = zplanes[0, p]
        for i in range(1, ngz):
            plane = plane + zplanes[i, p]
        ext[p, own, :] = plane
        packed = jnp.where(lax.shift_right_logical(lane, 4) == p, pltpu.roll(plane, 2 * HALO * p + HALO, 1), packed)
    cxsend[...] = packed

    low, high = slice(0, HALO), slice(ny - HALO, ny)
    elow, ehigh = slice(0, HALO), slice(HALO + ny, 2 * HALO + ny)
    coarse = []
    for s, (dy, dx) in enumerate(SIDES):
        rows = low if dy < 0 else high
        into = ehigh if dy < 0 else elow
        if dx == 0:
            src, dst = ext.at[:, slice(rows.start + HALO, rows.stop + HALO)], ext.at[:, into]
        elif dy == 0:
            src, dst = cxsend, cxrecv.at[0 if dx > 0 else 1, own]
        else:
            src, dst = cxsend.at[rows], cxrecv.at[0 if dx > 0 else 1, into]
        coarse.append((exists(dy, dx), exists(-dy, -dx), remote(src, dst, c_send.at[s], c_recv.at[s], at(dy, dx))))
    pl.semaphore_wait(near_sem, count)
    start(coarse)
    loop(half, nz, solve, 0, 2)
    wait_recv(coarse)

    rows = ny + 2 * HALO
    elane = lax.broadcasted_iota(jnp.int32, (rows, nx), 1)
    efirst, elast = elane == 0, elane == nx - 1
    near = jnp.logical_or(elane < HALO, elane >= nx - HALO)
    beside = jnp.where(lax.rem(elane, 2 * HALO) < HALO, cxrecv[0], cxrecv[1])
    a = [ext[p] for p in range(PLANES)]
    b = [jnp.where(near, pltpu.roll(beside, nx - (2 * HALO * p + HALO), 1), 0.0) for p in range(PLANES)]

    def east(a, b):
        ra, rb = pltpu.roll(a, nx - 1, 1), pltpu.roll(b, nx - 1, 1)
        return jnp.where(elast, rb, ra), jnp.where(elast, ra, rb)

    def west(a, b):
        ra, rb = pltpu.roll(a, 1, 1), pltpu.roll(b, 1, 1)
        return jnp.where(efirst, rb, ra), jnp.where(efirst, ra, rb)

    mid = slice(HALO, HALO + rows)
    wests = west(a[3], b[3])
    terms = []
    for s, planes in enumerate((a, b)):
        there = planes[1] > 0.0
        inv = jnp.where(there, RELAX / jnp.where(there, planes[1], 1.0), 0.0)
        field[s, mid, :] = planes[2]
        south = field[s, HALO - 1:HALO - 1 + rows, :]
        terms.append((planes[0] * inv, planes[2] * inv, south * inv, planes[3] * inv, wests[s] * inv))

    c = [terms[0][0], terms[1][0]]
    for sweep in range(1, SWEEPS):
        e, ws = east(*c), west(*c)
        for s in range(2):
            field[s, mid, :] = c[s]
        nxt = []
        for s in range(2):
            r, tyn, tys, txe, txw = terms[s]
            nxt.append((1.0 - RELAX) * c[s] + r
                       + tyn * field[s, HALO + 1:HALO + 1 + rows, :] + tys * field[s, HALO - 1:HALO - 1 + rows, :]
                       + txe * e[s] + txw * ws[s])
        c = nxt
    e, ws = east(*c), west(*c)
    final[0] = c[0]
    final[1] = e[0]
    final[2] = ws[0]
    wait_send(halos)
    for copy in sums:
        copy.wait_send()
    wait_send(coarse)


def finish_kernel(parts, w, qv, tzs, ty, txp, txm, final, new_hbm, corr_ref, out, out_sem):
    nz, ny, nx = tzs.shape
    own = slice(HALO, HALO + ny)
    cc, ce, cw = (final[k, own, :] for k in range(3))
    cn, cs = final[0, HALO + 1:HALO + 1 + ny, :], final[0, HALO - 1:HALO - 1 + ny, :]
    corr_ref[...] = cc

    def finish(z, _):
        g = (tzs[z] * cc + ty[z, own, :] * cn + ty[z, HALO - 1:HALO + ny - 1, :] * cs
             + txp[z] * ce + txm[z] * cw)
        for r in range(3):
            out[r, z] = w[r, z] + qv[r, z] * g
        return 0

    step = nz // parts
    outs = []
    for part in range(parts):
        lax.fori_loop(part * step, (part + 1) * step, finish, 0)
        chunk = slice(part * step, (part + 1) * step)
        outs.append(pltpu.make_async_copy(out.at[:, chunk], new_hbm.at[:, chunk], out_sem.at[part]))
        outs[-1].start()
    for copy in outs:
        copy.wait()


def per_device(sizes, state, right_side, permeability, pore_volume, facies, storage_table, coupling_table):
    _, nz, ny, nx = state.shape
    sizes = sizes + (nz, ny, nx)
    f32 = jnp.float32
    ngz = sizes[2]
    cells = (nz, ny, nx)
    vmem = lambda *shape: pltpu.VMEM(shape, f32)
    hbm = pl.BlockSpec(memory_space=pltpu.HBM)
    dma = lambda n: pltpu.SemaphoreType.DMA((n,))
    ey = ny + 2 * HALO
    facets = storage_table.shape[0]
    in_vmem = pl.BlockSpec(memory_space=pltpu.VMEM)
    handed = 4 * nx * (9 * nz * ny + nz * ey + 3 * ey)
    limit = 16384 * ((VMEM_BYTES - handed) // 16384)
    middle = pl.pallas_call(
        functools.partial(kernel, sizes),
        out_shape=(vmem(3, *cells), vmem(3, *cells), vmem(*cells), vmem(nz, ey, nx), vmem(*cells), vmem(*cells),
                   vmem(3, ey, nx)),
        in_specs=[hbm, hbm, hbm, hbm, hbm, hbm, hbm],
        out_specs=(in_vmem,) * 7,
        scratch_shapes=[
            vmem(4, nz + 2, ey, nx), vmem(3, *cells),
            pltpu.VMEM(cells, permeability.dtype), pltpu.VMEM(cells, pore_volume.dtype),
            vmem(2, 4 * nz, nx), vmem(2, 4 * nz, nx), vmem(ny, nx), vmem(2, ny, nx),
            vmem(2, 4, ny, nx), vmem(2, 4 * nz, nx), vmem(4 * nz, nx),
            vmem(3, *cells), vmem(*cells),
            vmem(ngz, PLANES, ny, nx), vmem(PLANES, ey, nx),
            vmem(ny, nx), vmem(2, ey, nx), vmem(2, ey + 2 * HALO, nx),
            pltpu.SMEM((nz,), facies.dtype), pltpu.SMEM((3, facets, 3), f32), pltpu.SMEM((3, facets, 3), f32),
            pltpu.SemaphoreType.REGULAR, dma(7), dma(6), dma(6), dma(max(ngz - 1, 1)), dma(ngz), dma(8), dma(8),
        ],
        compiler_params=pltpu.CompilerParams(collective_id=0, has_side_effects=True, vmem_limit_bytes=limit),
        name="cpr_apply",
    )(facies, storage_table.transpose(1, 0, 2), coupling_table.transpose(1, 0, 2),
      state, right_side, permeability, pore_volume)
    parts = 4
    return tuple(pl.pallas_call(
        functools.partial(finish_kernel, parts),
        out_shape=(jax.ShapeDtypeStruct(state.shape, f32), jax.ShapeDtypeStruct((ny, nx), f32)),
        in_specs=[in_vmem] * 7,
        out_specs=(hbm, in_vmem),
        scratch_shapes=[vmem(3, *cells), dma(parts)],
        compiler_params=pltpu.CompilerParams(vmem_limit_bytes=16 * 2**20),
        name="cpr_finish",
    )(*middle))


def solution(mesh):
    sizes = (mesh.shape["gx"], mesh.shape["gy"], mesh.shape["gz"])
    return jax.shard_map(
        functools.partial(per_device, sizes),
        mesh=mesh,
        in_specs=(
            P(None, "gz", "gy", "gx"),
            P(None, "gz", "gy", "gx"),
            P("gz", "gy", "gx"),
            P("gz", "gy", "gx"),
            P("gz"),
            P(),
            P(),
        ),
        out_specs=(P(None, "gz", "gy", "gx"), P("gy", "gx")),
        check_vma=False,
    )
```

```python
import functools
import jax
import jax.numpy as jnp
from jax import lax
from jax.experimental import pallas as pl
from jax.experimental.pallas import tpu as pltpu
from jax.sharding import PartitionSpec as P

SWEEPS = 8
RELAX = 0.8
MESH = pl.DeviceIdType.MESH
HALO = 8
VMEM_BYTES = 67043328

PLANES = 4
SIDES = [(-1, 0), (1, 0), (0, -1), (0, 1), (-1, -1), (-1, 1), (1, -1), (1, 1)]


def face(a, b):
    return 2.0 * a * b / (a + b)


def upper_rows(ny):
    return HALO * (-(-ny // (2 * HALO)))


def kernel(sizes, facies_hbm, mtab_hbm, ktab_hbm, state_hbm, rhs_hbm, perm_hbm, pore_hbm,
           w, qv, tzs, ty, txp, txm, final,
           u, rhs, permb, poreb, ysend, yrecv, xsend, xrecv, zrecv, yedge, rowk,
           flux, tot, zplanes, ext, cxsend, cxrecv, field,
           facies, mtab, ktab, near_sem, in_sem, h_send, h_recv, z_send, z_recv, c_send, c_recv):
    ngx, ngy, ngz, nz, ny, nx = sizes
    ix, iy, iz = lax.axis_index("gx"), lax.axis_index("gy"), lax.axis_index("gz")
    own = slice(HALO, HALO + ny)
    split = upper_rows(ny)

    def exists(dy, dx):
        ok = None
        for d, i, n in ((dy, iy, ngy), (dx, ix, ngx)):
            if d:
                here = (i > 0) if d < 0 else (i < n - 1)
                ok = here if ok is None else jnp.logical_and(ok, here)
        return ok

    def at(dy, dx):
        return {"gx": ix + dx, "gy": iy + dy, "gz": iz}

    barrier = pltpu.get_barrier_semaphore()
    for side in SIDES[:4]:
        @pl.when(exists(*side))
        def _(side=side):
            pl.semaphore_signal(barrier, inc=1, device_id=at(*side), device_id_type=MESH)
    for d in range(1, ngz):
        pl.semaphore_signal(barrier, inc=1, device_id={"gx": ix, "gy": iy, "gz": lax.rem(iz + d, ngz)},
                            device_id_type=MESH)

    loads = [
        pltpu.make_async_copy(perm_hbm, permb, in_sem.at[0]),
        pltpu.make_async_copy(state_hbm, u.at[0:3, 1:nz + 1, own], in_sem.at[1]),
        pltpu.make_async_copy(pore_hbm, poreb, in_sem.at[2]),
        pltpu.make_async_copy(rhs_hbm, rhs, in_sem.at[3]),
        pltpu.make_async_copy(facies_hbm, facies, in_sem.at[4]),
        pltpu.make_async_copy(mtab_hbm, mtab, in_sem.at[5]),
        pltpu.make_async_copy(ktab_hbm, ktab, in_sem.at[6]),
    ]
    for load in loads:
        load.start()

    lane = lax.broadcasted_iota(jnp.int32, (ny, nx), 1)

    def zero(ref):
        ref[...] = jnp.zeros(ref.shape, ref.dtype)

    for cond, refs in (
        (iz == 0, [zrecv.at[0]]),
        (iz == ngz - 1, [zrecv.at[1]]),
        (iy == 0, [yrecv.at[:, 0], ext.at[:, 0:HALO]]),
        (iy == ngy - 1, [yrecv.at[:, 1], ext.at[:, HALO + ny:]]),
        (ix == 0, [xrecv.at[:, 0], cxrecv.at[0, own]]),
        (ix == ngx - 1, [xrecv.at[:, 1], cxrecv.at[1, own]]),
        (jnp.logical_or(iy == 0, ix == 0), [cxrecv.at[0, 0:HALO]]),
        (jnp.logical_or(iy == 0, ix == ngx - 1), [cxrecv.at[1, 0:HALO]]),
        (jnp.logical_or(iy == ngy - 1, ix == 0), [cxrecv.at[0, HALO + ny:]]),
        (jnp.logical_or(iy == ngy - 1, ix == ngx - 1), [cxrecv.at[1, HALO + ny:]]),
    ):
        @pl.when(cond)
        def _(refs=refs):
            for ref in refs:
                zero(ref)
    zero(field)
    zero(u.at[:, nz + 1, own])
    zero(u.at[:, 0, own])

    loads[0].wait()
    for load in loads[4:]:
        load.wait()

    def loop(begin, end, body, carry, unroll):
        def several(i, carry):
            for k in range(unroll):
                carry = body(begin + i * unroll + k, carry)
            return carry
        return lax.fori_loop(0, (end - begin) // unroll, several, carry)

    def coefficient(table, z, r, c):
        return table[r, facies[z], c]

    def widen(z, _):
        u[3, z + 1, own, :] = permb[z].astype(jnp.float32)
        for k in range(4):
            u[k, z + 1, 0:HALO, :] = jnp.zeros((HALO, nx), jnp.float32)
            u[k, z + 1, HALO + ny:, :] = jnp.zeros((HALO, nx), jnp.float32)
        rowk[pl.ds(z, 1), :] = jnp.full((1, nx), coefficient(ktab, z, 0, 0), jnp.float32)
        return 0

    loop(0, nz, widen, 0, 2)
    loads[1].wait()

    def pair(batch, z, part):
        if batch:
            return part(1), part(2)
        return sum(coefficient(ktab, z, 0, k) * part(k) for k in range(3)), part(3)

    def pack_rows(batch):
        def body(z, _):
            for side, at_row in ((0, HALO), (1, HALO + ny - 1)):
                for i, x in enumerate(pair(batch, z, lambda k: u[k, z + 1, at_row:at_row + 1, :])):
                    ysend[batch, side, pl.ds(i * nz + z, 1), :] = x
            return 0

        loop(0, nz, body, 0, 4)

    pack_rows(0)

    count = sum(exists(*side).astype(jnp.int32) for side in SIDES[:4])
    pl.semaphore_wait(barrier, count + (ngz - 1))
    for side in SIDES[:4]:
        @pl.when(exists(*side))
        def _(side=side):
            pl.semaphore_signal(near_sem, inc=1, device_id=at(*side), device_id_type=MESH)

    def remote(src, dst, send, recv, device):
        return pltpu.make_async_remote_copy(src_ref=src, dst_ref=dst, send_sem=send, recv_sem=recv,
                                            device_id=device, device_id_type=MESH)

    def z_device(d):
        return {"gx": ix, "gy": iy, "gz": iz + d}

    halos = [
        (iz < ngz - 1, iz > 0, remote(u.at[:, nz, own], zrecv.at[0], h_send.at[0], h_recv.at[0], z_device(1))),
        (iz > 0, iz < ngz - 1, remote(u.at[:, 1, own], zrecv.at[1], h_send.at[1], h_recv.at[1], z_device(-1))),
        (exists(1, 0), exists(-1, 0), remote(ysend.at[0, 1], yrecv.at[0, 0], h_send.at[2], h_recv.at[2], at(1, 0))),
        (exists(-1, 0), exists(1, 0), remote(ysend.at[0, 0], yrecv.at[0, 1], h_send.at[3], h_recv.at[3], at(-1, 0))),
        (exists(0, 1), exists(0, -1), remote(xsend.at[0], xrecv.at[0, 0], h_send.at[4], h_recv.at[4], at(0, 1))),
        (exists(0, -1), exists(0, 1), remote(xsend.at[0], xrecv.at[0, 1], h_send.at[5], h_recv.at[5], at(0, -1))),
    ]
    rest = [
        (exists(1, 0), exists(-1, 0), remote(ysend.at[1, 1], yrecv.at[1, 0], h_send.at[6], h_recv.at[6], at(1, 0))),
        (exists(-1, 0), exists(1, 0), remote(ysend.at[1, 0], yrecv.at[1, 1], h_send.at[7], h_recv.at[7], at(-1, 0))),
        (exists(0, 1), exists(0, -1), remote(xsend.at[1], xrecv.at[1, 0], h_send.at[8], h_recv.at[8], at(0, 1))),
        (exists(0, -1), exists(0, 1), remote(xsend.at[1], xrecv.at[1, 1], h_send.at[9], h_recv.at[9], at(0, -1))),
    ]

    def start(copies):
        for sends, _, copy in copies:
            @pl.when(sends)
            def _(copy=copy):
                copy.start()

    def wait_recv(copies):
        for _, gets, copy in copies:
            @pl.when(gets)
            def _(copy=copy):
                copy.wait_recv()

    def wait_send(copies):
        for sends, _, copy in copies:
            @pl.when(sends)
            def _(copy=copy):
                copy.wait_send()

    start(halos[:4])

    half = nx // 2
    lane_pair = lax.shift_right_logical(lane, 1)
    nil = jnp.zeros((ny, nx), jnp.float32)

    def pack_columns(batch):
        def body(z, carry):
            packed, lanek = carry
            for i, x in enumerate(pair(batch, z, lambda k: u[k, z + 1, own, :])):
                j = i * nz + z
                upper = pltpu.roll(x[:split], 2 * j + 1, 1)
                lower = pltpu.roll(x[split:], lax.rem(2 * j + 1 + half, nx), 1)
                packed = jnp.where(lane_pair[:split] == j, upper, packed)
                beside = jnp.where(lane_pair[:ny - split] == j + half // 2, lower, packed[:ny - split])
                packed = beside if ny == 2 * split else jnp.concatenate([beside, packed[ny - split:]], axis=0)
            lanek = jnp.where(lane_pair[0:1] == nz + z, coefficient(ktab, z, 0, 0), lanek)
            return packed, lanek

        packed, lanek = loop(0, nz, body, (nil[:split], nil[0:1]), 4)
        xsend[batch] = packed
        return lanek

    def unpacked(x):
        return jnp.concatenate([x, pltpu.roll(x[:ny - split], half, 1)], axis=0)

    lanek = pack_columns(0)
    start(halos[4:])
    pack_rows(1)
    pack_columns(1)
    start(rest)
    loads[2].wait()
    loads[3].wait()

    first, last = lane == 0, lane == nx - 1

    def assemble(z, carry):
        tzm, s_rhs, s_diag, s_ty, s_tx = carry
        q = u[3, z + 1, own, :]
        tzp = face(q, u[3, z + 2, own, :])
        typ = face(q, u[3, z + 1, HALO + 1:HALO + ny + 1, :])
        ty[z, own, :] = typ
        ty[z, 0:HALO, :] = jnp.zeros((HALO, nx), jnp.float32)
        tym = ty[z, HALO - 1:HALO + ny - 1, :]
        xp = jnp.where(last, 0.0, face(q, pltpu.roll(q, nx - 1, 1)))
        xm = pltpu.roll(xp, 1, 1)
        txp[z] = xp
        txm[z] = xm
        tz = tzp + tzm
        areal = typ + tym + xp + xm
        tzs[z] = tz
        tot[z] = tz + areal
        v = poreb[z].astype(jnp.float32)
        local, moved = 0.0, 0.0
        for k in range(3):
            c = u[k, z + 1, own, :]
            f = (tzp * (c - u[k, z + 2, own, :]) + tzm * (c - u[k, z, own, :])
                 + typ * (c - u[k, z + 1, HALO + 1:HALO + ny + 1, :])
                 + tym * (c - u[k, z + 1, HALO - 1:HALO + ny - 1, :])
                 + xp * (c - pltpu.roll(c, nx - 1, 1)) + xm * (c - pltpu.roll(c, 1, 1)))
            flux[k, z] = f
            local = local + coefficient(mtab, z, 0, k) * c
            moved = moved + coefficient(ktab, z, 0, k) * f
        res = rhs[0, z] - (v * local + moved)
        k00 = coefficient(ktab, z, 0, 0)
        return (tzp, s_rhs + res, s_diag + (v * coefficient(mtab, z, 0, 0) + k00 * areal),
                s_ty + k00 * typ, s_tx + k00 * xp)

    _, s_rhs, s_diag, s_ty, s_tx = loop(0, nz, assemble, (nil,) * 5, 2)
    wait_recv(halos)

    for side, z in ((0, 0), (1, nz - 1)):
        t = face(u[3, z + 1, own, :], zrecv[side, 3])
        for k in range(3):
            f = t * (u[k, z + 1, own, :] - zrecv[side, k])
            flux[k, z] = flux[k, z] + f
            s_rhs = s_rhs - coefficient(ktab, z, 0, k) * f
        tzs[z] = tzs[z] + t
        tot[z] = tot[z] + t

    row = lax.broadcasted_iota(jnp.int32, (ny, nx), 0)
    for side, at_row in ((0, 0), (1, ny - 1)):
        t = face(ysend[0, side, nz:, :], yrecv[0, side, nz:, :])
        f = t * (ysend[0, side, :nz, :] - yrecv[0, side, :nz, :])
        yedge[side, 0:nz, :] = f
        yedge[side, 3 * nz:, :] = t
        moved = jnp.sum(f, axis=0, keepdims=True)
        weight = jnp.sum(rowk[...] * t, axis=0, keepdims=True)
        here = row == at_row
        s_rhs = s_rhs - jnp.where(here, moved, 0.0)
        s_diag = s_diag + jnp.where(here, weight, 0.0)
        if side:
            s_ty = s_ty + jnp.where(here, weight, 0.0)

    even = lax.rem(lane, 2) == 0
    low_at = jnp.logical_and(even, lane < 2 * nz)
    high_at = jnp.logical_and(even, jnp.logical_and(lane >= 2 * nz, lane < 4 * nz))

    def columns(batch, side):
        mine, other = unpacked(xsend[batch]), unpacked(xrecv[batch, side])
        if side:
            return mine, pltpu.roll(other, nx - 1, 1)
        return pltpu.roll(mine, nx - 1, 1), other

    def merged(edges):
        return jnp.where(even, edges[0], pltpu.roll(edges[1], nx - 1, 1))

    edges, spread = [], []
    for side, edge in ((0, first), (1, last)):
        here, there = columns(0, side)
        t = jnp.where(high_at, face(jnp.where(high_at, here, 1.0), jnp.where(high_at, there, 1.0)), 0.0)
        down = pltpu.roll(t, nx - 2 * nz, 1)
        f = jnp.where(low_at, down * (here - there), 0.0)
        moved = jnp.sum(f, axis=1, keepdims=True)
        weight = jnp.sum(t * lanek, axis=1, keepdims=True)
        s_rhs = s_rhs - jnp.where(edge, moved, 0.0)
        s_diag = s_diag + jnp.where(edge, weight, 0.0)
        if side:
            s_tx = s_tx + jnp.where(edge, weight, 0.0)
        edges.append(f + t)
        spread.append(down + t)
    border = merged(edges)

    for p, plane in enumerate((s_rhs, s_diag, s_ty, s_tx)):
        zplanes[iz, p] = plane

    others = [lax.rem(iz + d, ngz) for d in range(1, ngz)]
    sums = [remote(zplanes.at[iz], zplanes.at[iz], z_send.at[d], z_recv.at[iz], {"gx": ix, "gy": iy, "gz": peer})
            for d, peer in enumerate(others)]
    for copy in sums:
        copy.start()

    outer = jnp.logical_or(first, last)

    def solve(z, _):
        v = poreb[z].astype(jnp.float32)
        k01, k02 = coefficient(ktab, z, 0, 1), coefficient(ktab, z, 0, 2)
        inv_k00 = 1.0 / rowk[pl.ds(z, 1), :]
        for side, at_row in ((0, 0), (1, ny - 1)):
            here = slice(at_row, at_row + 1)
            coarse_row, one, two, t = (yedge[side, pl.ds(k * nz + z, 1), :] for k in range(4))
            zero_row = (coarse_row - k01 * one - k02 * two) * inv_k00
            for k, x in enumerate((zero_row, one, two)):
                flux[k, z, here, :] = flux[k, z, here, :] + x
            tot[z, here, :] = tot[z, here, :] + t
            at_face = HALO - 1 + side * ny
            ty[z, at_face:at_face + 1, :] = t

        def beside(values, j):
            return jnp.where(outer, pltpu.roll(values, lax.rem(2 * nx - 2 * j, nx), 1), 0.0)

        one, two = beside(border_rest, z), beside(border_rest, nz + z)
        added = [(beside(border, z) - k01 * one - k02 * two) * inv_k00, one, two]
        t = beside(border, nz + z)
        txp[z] = txp[z] + jnp.where(last, t, 0.0)
        txm[z] = txm[z] + jnp.where(first, t, 0.0)
        total = tot[z] + t
        m = [[coefficient(mtab, z, r, c) for c in range(3)] for r in range(3)]
        kk = [[coefficient(ktab, z, r, c) for c in range(3)] for r in range(3)]
        e = [[v * m[r][c] + total * kk[r][c] for c in range(3)] for r in range(3)]

        def cofactor(r, c):
            return (e[(r + 1) % 3][(c + 1) % 3] * e[(r + 2) % 3][(c + 2) % 3]
                    - e[(r + 1) % 3][(c + 2) % 3] * e[(r + 2) % 3][(c + 1) % 3])

        cells = [u[k, z + 1, own, :] for k in range(3)]
        f = [flux[k, z] + added[k] for k in range(3)]
        res = []
        for r in range(3):
            res.append(rhs[r, z] - (v * (m[r][0] * cells[0] + m[r][1] * cells[1] + m[r][2] * cells[2])
                                    + (kk[r][0] * f[0] + kk[r][1] * f[1] + kk[r][2] * f[2])))
        fac = [[cofactor(r, c) for c in range(3)] for r in range(3)]
        inv = 1.0 / (e[0][0] * fac[0][0] + e[0][1] * fac[0][1] + e[0][2] * fac[0][2])
        for r in range(3):
            w[r, z] = cells[r] + (fac[0][r] * res[0] + fac[1][r] * res[1] + fac[2][r] * res[2]) * inv
            qv[r, z] = (fac[0][r] * kk[0][0] + fac[1][r] * kk[1][0] + fac[2][r] * kk[2][0]) * inv
        return 0

    for peer in others:
        remote(zplanes.at[peer], zplanes.at[peer], z_send.at[0], z_recv.at[peer],
               {"gx": ix, "gy": iy, "gz": peer}).wait_recv()
    packed = nil
    for p in range(PLANES):
        plane = zplanes[0, p]
        for i in range(1, ngz):
            plane = plane + zplanes[i, p]
        ext[p, own, :] = plane
        packed = jnp.where(lax.shift_right_logical(lane, 4) == p, pltpu.roll(plane, 2 * HALO * p + HALO, 1), packed)
    cxsend[...] = packed

    low, high = slice(0, HALO), slice(ny - HALO, ny)
    elow, ehigh = slice(0, HALO), slice(HALO + ny, 2 * HALO + ny)
    coarse = []
    for s, (dy, dx) in enumerate(SIDES):
        rows = low if dy < 0 else high
        into = ehigh if dy < 0 else elow
        if dx == 0:
            src, dst = ext.at[:, slice(rows.start + HALO, rows.stop + HALO)], ext.at[:, into]
        elif dy == 0:
            src, dst = cxsend, cxrecv.at[0 if dx > 0 else 1, own]
        else:
            src, dst = cxsend.at[rows], cxrecv.at[0 if dx > 0 else 1, into]
        coarse.append((exists(dy, dx), exists(-dy, -dx), remote(src, dst, c_send.at[s], c_recv.at[s], at(dy, dx))))
    pl.semaphore_wait(near_sem, count)
    start(coarse)
    wait_recv(rest)
    for side in range(2):
        t = yedge[side, 3 * nz:, :]
        for i in range(2):
            part = slice(i * nz, (i + 1) * nz)
            yedge[side, (i + 1) * nz:(i + 2) * nz, :] = t * (ysend[1, side, part, :] - yrecv[1, side, part, :])
    edges = []
    for side in range(2):
        here, there = columns(1, side)
        edges.append(jnp.where(lane < 4 * nz, spread[side] * (here - there), 0.0))
    border_rest = merged(edges)
    loop(0, nz, solve, 0, 2)
    wait_recv(coarse)

    rows = ny + 2 * HALO
    elane = lax.broadcasted_iota(jnp.int32, (rows, nx), 1)
    efirst, elast = elane == 0, elane == nx - 1
    near = jnp.logical_or(elane < HALO, elane >= nx - HALO)
    beside = jnp.where(lax.rem(elane, 2 * HALO) < HALO, cxrecv[0], cxrecv[1])
    a = [ext[p] for p in range(PLANES)]
    b = [jnp.where(near, pltpu.roll(beside, nx - (2 * HALO * p + HALO), 1), 0.0) for p in range(PLANES)]

    def east(a, b):
        ra, rb = pltpu.roll(a, nx - 1, 1), pltpu.roll(b, nx - 1, 1)
        return jnp.where(elast, rb, ra), jnp.where(elast, ra, rb)

    def west(a, b):
        ra, rb = pltpu.roll(a, 1, 1), pltpu.roll(b, 1, 1)
        return jnp.where(efirst, rb, ra), jnp.where(efirst, ra, rb)

    mid = slice(HALO, HALO + rows)
    wests = west(a[3], b[3])
    terms = []
    for s, planes in enumerate((a, b)):
        there = planes[1] > 0.0
        inv = jnp.where(there, RELAX / jnp.where(there, planes[1], 1.0), 0.0)
        field[s, mid, :] = planes[2]
        south = field[s, HALO - 1:HALO - 1 + rows, :]
        terms.append((planes[0] * inv, planes[2] * inv, south * inv, planes[3] * inv, wests[s] * inv))

    c = [terms[0][0], terms[1][0]]
    for sweep in range(1, SWEEPS):
        e, ws = east(*c), west(*c)
        for s in range(2):
            field[s, mid, :] = c[s]
        nxt = []
        for s in range(2):
            r, tyn, tys, txe, txw = terms[s]
            nxt.append((1.0 - RELAX) * c[s] + r
                       + tyn * field[s, HALO + 1:HALO + 1 + rows, :] + tys * field[s, HALO - 1:HALO - 1 + rows, :]
                       + txe * e[s] + txw * ws[s])
        c = nxt
    e, ws = east(*c), west(*c)
    final[0] = c[0]
    final[1] = e[0]
    final[2] = ws[0]
    wait_send(halos + rest)
    for copy in sums:
        copy.wait_send()
    wait_send(coarse)


def finish_kernel(parts, w, qv, tzs, ty, txp, txm, final, new_hbm, corr_ref, out, out_sem):
    nz, ny, nx = tzs.shape
    own = slice(HALO, HALO + ny)
    cc, ce, cw = (final[k, own, :] for k in range(3))
    cn, cs = final[0, HALO + 1:HALO + 1 + ny, :], final[0, HALO - 1:HALO - 1 + ny, :]
    corr_ref[...] = cc

    def finish(z, _):
        g = (tzs[z] * cc + ty[z, own, :] * cn + ty[z, HALO - 1:HALO + ny - 1, :] * cs
             + txp[z] * ce + txm[z] * cw)
        for r in range(3):
            out[r, z] = w[r, z] + qv[r, z] * g
        return 0

    step = nz // parts
    outs = []
    for part in range(parts):
        lax.fori_loop(part * step, (part + 1) * step, finish, 0)
        chunk = slice(part * step, (part + 1) * step)
        outs.append(pltpu.make_async_copy(out.at[:, chunk], new_hbm.at[:, chunk], out_sem.at[part]))
        outs[-1].start()
    for copy in outs:
        copy.wait()


def per_device(sizes, state, right_side, permeability, pore_volume, facies, storage_table, coupling_table):
    _, nz, ny, nx = state.shape
    sizes = sizes + (nz, ny, nx)
    f32 = jnp.float32
    ngz = sizes[2]
    cells = (nz, ny, nx)
    vmem = lambda *shape: pltpu.VMEM(shape, f32)
    hbm = pl.BlockSpec(memory_space=pltpu.HBM)
    dma = lambda n: pltpu.SemaphoreType.DMA((n,))
    ey = ny + 2 * HALO
    split = upper_rows(ny)
    facets = storage_table.shape[0]
    in_vmem = pl.BlockSpec(memory_space=pltpu.VMEM)
    handed = 4 * nx * (9 * nz * ny + nz * ey + 3 * ey)
    limit = 16384 * ((VMEM_BYTES - handed) // 16384)
    middle = pl.pallas_call(
        functools.partial(kernel, sizes),
        out_shape=(vmem(3, *cells), vmem(3, *cells), vmem(*cells), vmem(nz, ey, nx), vmem(*cells), vmem(*cells),
                   vmem(3, ey, nx)),
        in_specs=[hbm, hbm, hbm, hbm, hbm, hbm, hbm],
        out_specs=(in_vmem,) * 7,
        scratch_shapes=[
            vmem(4, nz + 2, ey, nx), vmem(3, *cells),
            pltpu.VMEM(cells, permeability.dtype), pltpu.VMEM(cells, pore_volume.dtype),
            vmem(2, 2, 2 * nz, nx), vmem(2, 2, 2 * nz, nx), vmem(2, split, nx), vmem(2, 2, split, nx),
            vmem(2, 4, ny, nx), vmem(2, 4 * nz, nx), vmem(nz, nx),
            vmem(3, *cells), vmem(*cells),
            vmem(ngz, PLANES, ny, nx), vmem(PLANES, ey, nx),
            vmem(ny, nx), vmem(2, ey, nx), vmem(2, ey + 2 * HALO, nx),
            pltpu.SMEM((nz,), facies.dtype), pltpu.SMEM((3, facets, 3), f32), pltpu.SMEM((3, facets, 3), f32),
            pltpu.SemaphoreType.REGULAR, dma(7), dma(10), dma(10), dma(max(ngz - 1, 1)), dma(ngz), dma(8), dma(8),
        ],
        compiler_params=pltpu.CompilerParams(collective_id=0, has_side_effects=True, vmem_limit_bytes=limit),
        name="cpr_apply",
    )(facies, storage_table.transpose(1, 0, 2), coupling_table.transpose(1, 0, 2),
      state, right_side, permeability, pore_volume)
    parts = 4
    return tuple(pl.pallas_call(
        functools.partial(finish_kernel, parts),
        out_shape=(jax.ShapeDtypeStruct(state.shape, f32), jax.ShapeDtypeStruct((ny, nx), f32)),
        in_specs=[in_vmem] * 7,
        out_specs=(hbm, in_vmem),
        scratch_shapes=[vmem(3, *cells), dma(parts)],
        compiler_params=pltpu.CompilerParams(vmem_limit_bytes=16 * 2**20),
        name="cpr_finish",
    )(*middle))


def solution(mesh):
    sizes = (mesh.shape["gx"], mesh.shape["gy"], mesh.shape["gz"])
    return jax.shard_map(
        functools.partial(per_device, sizes),
        mesh=mesh,
        in_specs=(
            P(None, "gz", "gy", "gx"),
            P(None, "gz", "gy", "gx"),
            P("gz", "gy", "gx"),
            P("gz", "gy", "gx"),
            P("gz"),
            P(),
            P(),
        ),
        out_specs=(P(None, "gz", "gy", "gx"), P("gy", "gx")),
        check_vma=False,
    )
```

```python
import functools
import jax
import jax.numpy as jnp
from jax import lax
from jax.experimental import pallas as pl
from jax.experimental.pallas import tpu as pltpu
from jax.sharding import PartitionSpec as P

SWEEPS = 8
RELAX = 0.8
MESH = pl.DeviceIdType.MESH
HALO = 8
VMEM_BYTES = 67043328

PLANES = 4
SIDES = [(-1, 0), (1, 0), (0, -1), (0, 1), (-1, -1), (-1, 1), (1, -1), (1, 1)]


def face(a, b):
    return 2.0 * a * b / (a + b)


def upper_rows(ny):
    return HALO * (-(-ny // (2 * HALO)))


def kernel(sizes, facies_hbm, mtab_hbm, ktab_hbm, state_hbm, rhs_hbm, perm_hbm, pore_hbm,
           w, qv, tzs, ty, txp, txm, final,
           u, rhs, permb, poreb, ysend, yrecv, xsend, xrecv, zrecv, yedge, rowk,
           flux, tot, zplanes, ext, cxsend, cxrecv, cdrecv, field,
           facies, mtab, ktab, near_sem, in_sem, h_send, h_recv, z_send, z_recv, c_send, c_recv):
    ngx, ngy, ngz, nz, ny, nx = sizes
    ix, iy, iz = lax.axis_index("gx"), lax.axis_index("gy"), lax.axis_index("gz")
    own = slice(HALO, HALO + ny)
    split = upper_rows(ny)

    def exists(dy, dx):
        ok = None
        for d, i, n in ((dy, iy, ngy), (dx, ix, ngx)):
            if d:
                here = (i > 0) if d < 0 else (i < n - 1)
                ok = here if ok is None else jnp.logical_and(ok, here)
        return ok

    def at(dy, dx):
        return {"gx": ix + dx, "gy": iy + dy, "gz": iz}

    barrier = pltpu.get_barrier_semaphore()
    for side in SIDES[:4]:
        @pl.when(exists(*side))
        def _(side=side):
            pl.semaphore_signal(barrier, inc=1, device_id=at(*side), device_id_type=MESH)
    for d in range(1, ngz):
        pl.semaphore_signal(barrier, inc=1, device_id={"gx": ix, "gy": iy, "gz": lax.rem(iz + d, ngz)},
                            device_id_type=MESH)

    loads = [
        pltpu.make_async_copy(perm_hbm, permb, in_sem.at[0]),
        pltpu.make_async_copy(state_hbm, u.at[0:3, 1:nz + 1, own], in_sem.at[1]),
        pltpu.make_async_copy(pore_hbm, poreb, in_sem.at[2]),
        pltpu.make_async_copy(rhs_hbm, rhs, in_sem.at[3]),
        pltpu.make_async_copy(facies_hbm, facies, in_sem.at[4]),
        pltpu.make_async_copy(mtab_hbm, mtab, in_sem.at[5]),
        pltpu.make_async_copy(ktab_hbm, ktab, in_sem.at[6]),
    ]
    for load in loads:
        load.start()

    lane = lax.broadcasted_iota(jnp.int32, (ny, nx), 1)

    def zero(ref):
        ref[...] = jnp.zeros(ref.shape, ref.dtype)

    for cond, refs in (
        (iz == 0, [zrecv.at[0]]),
        (iz == ngz - 1, [zrecv.at[1]]),
        (iy == 0, [yrecv.at[:, 0], ext.at[:, 0:HALO]]),
        (iy == ngy - 1, [yrecv.at[:, 1], ext.at[:, HALO + ny:]]),
        (ix == 0, [xrecv.at[:, 0], cxrecv.at[0]]),
        (ix == ngx - 1, [xrecv.at[:, 1], cxrecv.at[1]]),
        (jnp.logical_or(iy == 0, ix == 0), [cdrecv.at[0, 0]]),
        (jnp.logical_or(iy == 0, ix == ngx - 1), [cdrecv.at[0, 1]]),
        (jnp.logical_or(iy == ngy - 1, ix == 0), [cdrecv.at[1, 0]]),
        (jnp.logical_or(iy == ngy - 1, ix == ngx - 1), [cdrecv.at[1, 1]]),
    ):
        @pl.when(cond)
        def _(refs=refs):
            for ref in refs:
                zero(ref)
    zero(field)
    zero(u.at[:, nz + 1, own])
    zero(u.at[:, 0, own])

    loads[0].wait()
    for load in loads[4:]:
        load.wait()

    def loop(begin, end, body, carry, unroll):
        def several(i, carry):
            for k in range(unroll):
                carry = body(begin + i * unroll + k, carry)
            return carry
        return lax.fori_loop(0, (end - begin) // unroll, several, carry)

    def coefficient(table, z, r, c):
        return table[r, facies[z], c]

    def widen(z, _):
        u[3, z + 1, own, :] = permb[z].astype(jnp.float32)
        for k in range(4):
            u[k, z + 1, 0:HALO, :] = jnp.zeros((HALO, nx), jnp.float32)
            u[k, z + 1, HALO + ny:, :] = jnp.zeros((HALO, nx), jnp.float32)
        rowk[pl.ds(z, 1), :] = jnp.full((1, nx), coefficient(ktab, z, 0, 0), jnp.float32)
        return 0

    loop(0, nz, widen, 0, 2)
    loads[1].wait()

    def pair(batch, z, part):
        if batch:
            return part(1), part(2)
        return sum(coefficient(ktab, z, 0, k) * part(k) for k in range(3)), part(3)

    def pack_rows(batch):
        def body(z, _):
            for side, at_row in ((0, HALO), (1, HALO + ny - 1)):
                for i, x in enumerate(pair(batch, z, lambda k: u[k, z + 1, at_row:at_row + 1, :])):
                    ysend[batch, side, pl.ds(i * nz + z, 1), :] = x
            return 0

        loop(0, nz, body, 0, 4)

    pack_rows(0)

    count = sum(exists(*side).astype(jnp.int32) for side in SIDES[:4])
    pl.semaphore_wait(barrier, count + (ngz - 1))
    for side in SIDES[:4]:
        @pl.when(exists(*side))
        def _(side=side):
            pl.semaphore_signal(near_sem, inc=1, device_id=at(*side), device_id_type=MESH)

    def remote(src, dst, send, recv, device):
        return pltpu.make_async_remote_copy(src_ref=src, dst_ref=dst, send_sem=send, recv_sem=recv,
                                            device_id=device, device_id_type=MESH)

    def z_device(d):
        return {"gx": ix, "gy": iy, "gz": iz + d}

    halos = [
        (iz < ngz - 1, iz > 0, remote(u.at[:, nz, own], zrecv.at[0], h_send.at[0], h_recv.at[0], z_device(1))),
        (iz > 0, iz < ngz - 1, remote(u.at[:, 1, own], zrecv.at[1], h_send.at[1], h_recv.at[1], z_device(-1))),
        (exists(1, 0), exists(-1, 0), remote(ysend.at[0, 1], yrecv.at[0, 0], h_send.at[2], h_recv.at[2], at(1, 0))),
        (exists(-1, 0), exists(1, 0), remote(ysend.at[0, 0], yrecv.at[0, 1], h_send.at[3], h_recv.at[3], at(-1, 0))),
        (exists(0, 1), exists(0, -1), remote(xsend.at[0], xrecv.at[0, 0], h_send.at[4], h_recv.at[4], at(0, 1))),
        (exists(0, -1), exists(0, 1), remote(xsend.at[0], xrecv.at[0, 1], h_send.at[5], h_recv.at[5], at(0, -1))),
    ]
    rest = [
        (exists(1, 0), exists(-1, 0), remote(ysend.at[1, 1], yrecv.at[1, 0], h_send.at[6], h_recv.at[6], at(1, 0))),
        (exists(-1, 0), exists(1, 0), remote(ysend.at[1, 0], yrecv.at[1, 1], h_send.at[7], h_recv.at[7], at(-1, 0))),
        (exists(0, 1), exists(0, -1), remote(xsend.at[1], xrecv.at[1, 0], h_send.at[8], h_recv.at[8], at(0, 1))),
        (exists(0, -1), exists(0, 1), remote(xsend.at[1], xrecv.at[1, 1], h_send.at[9], h_recv.at[9], at(0, -1))),
    ]

    def start(copies):
        for sends, _, copy in copies:
            @pl.when(sends)
            def _(copy=copy):
                copy.start()

    def wait_recv(copies):
        for _, gets, copy in copies:
            @pl.when(gets)
            def _(copy=copy):
                copy.wait_recv()

    def wait_send(copies):
        for sends, _, copy in copies:
            @pl.when(sends)
            def _(copy=copy):
                copy.wait_send()

    start(halos[:4])

    half = nx // 2
    lane_pair = lax.shift_right_logical(lane, 1)
    nil = jnp.zeros((ny, nx), jnp.float32)

    def pack_columns(batch):
        def body(z, carry):
            packed, lanek = carry
            for i, x in enumerate(pair(batch, z, lambda k: u[k, z + 1, own, :])):
                j = i * nz + z
                upper = pltpu.roll(x[:split], 2 * j + 1, 1)
                lower = pltpu.roll(x[split:], lax.rem(2 * j + 1 + half, nx), 1)
                packed = jnp.where(lane_pair[:split] == j, upper, packed)
                beside = jnp.where(lane_pair[:ny - split] == j + half // 2, lower, packed[:ny - split])
                packed = beside if ny == 2 * split else jnp.concatenate([beside, packed[ny - split:]], axis=0)
            lanek = jnp.where(lane_pair[0:1] == nz + z, coefficient(ktab, z, 0, 0), lanek)
            return packed, lanek

        packed, lanek = loop(0, nz, body, (nil[:split], nil[0:1]), 4)
        xsend[batch] = packed
        return lanek

    def unpacked(x):
        return jnp.concatenate([x, pltpu.roll(x[:ny - split], half, 1)], axis=0)

    lanek = pack_columns(0)
    start(halos[4:])
    pack_rows(1)
    pack_columns(1)
    start(rest)
    loads[2].wait()
    loads[3].wait()

    first, last = lane == 0, lane == nx - 1

    def assemble(z, carry):
        tzm, s_rhs, s_diag, s_ty, s_tx = carry
        q = u[3, z + 1, own, :]
        tzp = face(q, u[3, z + 2, own, :])
        typ = face(q, u[3, z + 1, HALO + 1:HALO + ny + 1, :])
        ty[z, own, :] = typ
        ty[z, 0:HALO, :] = jnp.zeros((HALO, nx), jnp.float32)
        tym = ty[z, HALO - 1:HALO + ny - 1, :]
        xp = jnp.where(last, 0.0, face(q, pltpu.roll(q, nx - 1, 1)))
        xm = pltpu.roll(xp, 1, 1)
        txp[z] = xp
        txm[z] = xm
        tz = tzp + tzm
        areal = typ + tym + xp + xm
        tzs[z] = tz
        tot[z] = tz + areal
        v = poreb[z].astype(jnp.float32)
        local, moved = 0.0, 0.0
        for k in range(3):
            c = u[k, z + 1, own, :]
            f = (tzp * (c - u[k, z + 2, own, :]) + tzm * (c - u[k, z, own, :])
                 + typ * (c - u[k, z + 1, HALO + 1:HALO + ny + 1, :])
                 + tym * (c - u[k, z + 1, HALO - 1:HALO + ny - 1, :])
                 + xp * (c - pltpu.roll(c, nx - 1, 1)) + xm * (c - pltpu.roll(c, 1, 1)))
            flux[k, z] = f
            local = local + coefficient(mtab, z, 0, k) * c
            moved = moved + coefficient(ktab, z, 0, k) * f
        res = rhs[0, z] - (v * local + moved)
        k00 = coefficient(ktab, z, 0, 0)
        return (tzp, s_rhs + res, s_diag + (v * coefficient(mtab, z, 0, 0) + k00 * areal),
                s_ty + k00 * typ, s_tx + k00 * xp)

    _, s_rhs, s_diag, s_ty, s_tx = loop(0, nz, assemble, (nil,) * 5, 2)
    wait_recv(halos)

    for side, z in ((0, 0), (1, nz - 1)):
        t = face(u[3, z + 1, own, :], zrecv[side, 3])
        for k in range(3):
            f = t * (u[k, z + 1, own, :] - zrecv[side, k])
            flux[k, z] = flux[k, z] + f
            s_rhs = s_rhs - coefficient(ktab, z, 0, k) * f
        tzs[z] = tzs[z] + t
        tot[z] = tot[z] + t

    row = lax.broadcasted_iota(jnp.int32, (ny, nx), 0)
    for side, at_row in ((0, 0), (1, ny - 1)):
        t = face(ysend[0, side, nz:, :], yrecv[0, side, nz:, :])
        f = t * (ysend[0, side, :nz, :] - yrecv[0, side, :nz, :])
        yedge[side, 0:nz, :] = f
        yedge[side, 3 * nz:, :] = t
        moved = jnp.sum(f, axis=0, keepdims=True)
        weight = jnp.sum(rowk[...] * t, axis=0, keepdims=True)
        here = row == at_row
        s_rhs = s_rhs - jnp.where(here, moved, 0.0)
        s_diag = s_diag + jnp.where(here, weight, 0.0)
        if side:
            s_ty = s_ty + jnp.where(here, weight, 0.0)

    even = lax.rem(lane, 2) == 0
    low_at = jnp.logical_and(even, lane < 2 * nz)
    high_at = jnp.logical_and(even, jnp.logical_and(lane >= 2 * nz, lane < 4 * nz))

    def columns(batch, side):
        mine, other = unpacked(xsend[batch]), unpacked(xrecv[batch, side])
        if side:
            return mine, pltpu.roll(other, nx - 1, 1)
        return pltpu.roll(mine, nx - 1, 1), other

    def merged(edges):
        return jnp.where(even, edges[0], pltpu.roll(edges[1], nx - 1, 1))

    edges, spread = [], []
    for side, edge in ((0, first), (1, last)):
        here, there = columns(0, side)
        t = jnp.where(high_at, face(jnp.where(high_at, here, 1.0), jnp.where(high_at, there, 1.0)), 0.0)
        down = pltpu.roll(t, nx - 2 * nz, 1)
        f = jnp.where(low_at, down * (here - there), 0.0)
        moved = jnp.sum(f, axis=1, keepdims=True)
        weight = jnp.sum(t * lanek, axis=1, keepdims=True)
        s_rhs = s_rhs - jnp.where(edge, moved, 0.0)
        s_diag = s_diag + jnp.where(edge, weight, 0.0)
        if side:
            s_tx = s_tx + jnp.where(edge, weight, 0.0)
        edges.append(f + t)
        spread.append(down + t)
    border = merged(edges)

    for p, plane in enumerate((s_rhs, s_diag, s_ty, s_tx)):
        zplanes[iz, p] = plane

    others = [lax.rem(iz + d, ngz) for d in range(1, ngz)]
    sums = [remote(zplanes.at[iz], zplanes.at[iz], z_send.at[d], z_recv.at[iz], {"gx": ix, "gy": iy, "gz": peer})
            for d, peer in enumerate(others)]
    for copy in sums:
        copy.start()

    outer = jnp.logical_or(first, last)

    def solve(z, _):
        v = poreb[z].astype(jnp.float32)
        k01, k02 = coefficient(ktab, z, 0, 1), coefficient(ktab, z, 0, 2)
        inv_k00 = 1.0 / rowk[pl.ds(z, 1), :]
        for side, at_row in ((0, 0), (1, ny - 1)):
            here = slice(at_row, at_row + 1)
            coarse_row, one, two, t = (yedge[side, pl.ds(k * nz + z, 1), :] for k in range(4))
            zero_row = (coarse_row - k01 * one - k02 * two) * inv_k00
            for k, x in enumerate((zero_row, one, two)):
                flux[k, z, here, :] = flux[k, z, here, :] + x
            tot[z, here, :] = tot[z, here, :] + t
            at_face = HALO - 1 + side * ny
            ty[z, at_face:at_face + 1, :] = t

        def beside(values, j):
            return jnp.where(outer, pltpu.roll(values, lax.rem(2 * nx - 2 * j, nx), 1), 0.0)

        one, two = beside(border_rest, z), beside(border_rest, nz + z)
        added = [(beside(border, z) - k01 * one - k02 * two) * inv_k00, one, two]
        t = beside(border, nz + z)
        txp[z] = txp[z] + jnp.where(last, t, 0.0)
        txm[z] = txm[z] + jnp.where(first, t, 0.0)
        total = tot[z] + t
        m = [[coefficient(mtab, z, r, c) for c in range(3)] for r in range(3)]
        kk = [[coefficient(ktab, z, r, c) for c in range(3)] for r in range(3)]
        e = [[v * m[r][c] + total * kk[r][c] for c in range(3)] for r in range(3)]

        def cofactor(r, c):
            return (e[(r + 1) % 3][(c + 1) % 3] * e[(r + 2) % 3][(c + 2) % 3]
                    - e[(r + 1) % 3][(c + 2) % 3] * e[(r + 2) % 3][(c + 1) % 3])

        cells = [u[k, z + 1, own, :] for k in range(3)]
        f = [flux[k, z] + added[k] for k in range(3)]
        res = []
        for r in range(3):
            res.append(rhs[r, z] - (v * (m[r][0] * cells[0] + m[r][1] * cells[1] + m[r][2] * cells[2])
                                    + (kk[r][0] * f[0] + kk[r][1] * f[1] + kk[r][2] * f[2])))
        fac = [[cofactor(r, c) for c in range(3)] for r in range(3)]
        inv = 1.0 / (e[0][0] * fac[0][0] + e[0][1] * fac[0][1] + e[0][2] * fac[0][2])
        for r in range(3):
            w[r, z] = cells[r] + (fac[0][r] * res[0] + fac[1][r] * res[1] + fac[2][r] * res[2]) * inv
            qv[r, z] = (fac[0][r] * kk[0][0] + fac[1][r] * kk[1][0] + fac[2][r] * kk[2][0]) * inv
        return 0

    for peer in others:
        remote(zplanes.at[peer], zplanes.at[peer], z_send.at[0], z_recv.at[peer],
               {"gx": ix, "gy": iy, "gz": peer}).wait_recv()
    slots = nx // (PLANES * HALO)
    groups = ny // HALO
    tiles = cxsend.shape[1]
    lane_group = lax.shift_right_logical(lane[:HALO], 3)
    packed = [[nil[:HALO]] * tiles for _ in range(2)]
    for p in range(PLANES):
        plane = zplanes[0, p]
        for i in range(1, ngz):
            plane = plane + zplanes[i, p]
        ext[p, own, :] = plane
        for g in range(groups):
            slot = (g % slots) * PLANES + p
            for side, shift in ((0, slot * HALO), (1, (slot + 1) * HALO)):
                moved = pltpu.roll(plane[g * HALO:(g + 1) * HALO], shift % nx, 1)
                packed[side][g // slots] = jnp.where(lane_group == slot, moved, packed[side][g // slots])
    for side in range(2):
        for tile in range(tiles):
            cxsend[side, tile] = packed[side][tile]

    low, high = slice(0, HALO), slice(ny - HALO, ny)
    elow, ehigh = slice(0, HALO), slice(HALO + ny, 2 * HALO + ny)
    coarse = []
    for s, (dy, dx) in enumerate(SIDES):
        rows = low if dy < 0 else high
        into = ehigh if dy < 0 else elow
        if dx == 0:
            src, dst = ext.at[:, slice(rows.start + HALO, rows.stop + HALO)], ext.at[:, into]
        elif dy == 0:
            src, dst = cxsend.at[(dx + 1) // 2], cxrecv.at[(1 - dx) // 2]
        else:
            tile = 0 if dy < 0 else (groups - 1) // slots
            src, dst = cxsend.at[(dx + 1) // 2, tile], cdrecv.at[(1 - dy) // 2, (1 - dx) // 2]
        coarse.append((exists(dy, dx), exists(-dy, -dx), remote(src, dst, c_send.at[s], c_recv.at[s], at(dy, dx))))
    pl.semaphore_wait(near_sem, count)
    start(coarse)
    wait_recv(rest)
    for side in range(2):
        t = yedge[side, 3 * nz:, :]
        for i in range(2):
            part = slice(i * nz, (i + 1) * nz)
            yedge[side, (i + 1) * nz:(i + 2) * nz, :] = t * (ysend[1, side, part, :] - yrecv[1, side, part, :])
    edges = []
    for side in range(2):
        here, there = columns(1, side)
        edges.append(jnp.where(lane < 4 * nz, spread[side] * (here - there), 0.0))
    border_rest = merged(edges)
    loop(0, nz, solve, 0, 2)
    wait_recv(coarse)

    rows = ny + 2 * HALO
    elane = lax.broadcasted_iota(jnp.int32, (rows, nx), 1)
    efirst, elast = elane == 0, elane == nx - 1
    a = [ext[p] for p in range(PLANES)]
    on_right, on_left = lane[:HALO] < HALO, lane[:HALO] >= nx - HALO

    def border_of(p, g):
        source = g % groups
        slot = (source % slots) * PLANES + p
        if 0 <= g < groups:
            from_left, from_right = cxrecv[0, g // slots], cxrecv[1, g // slots]
        else:
            from_left, from_right = cdrecv[0 if g < 0 else 1, 0], cdrecv[0 if g < 0 else 1, 1]
        back = (nx - slot * HALO) % nx
        return jnp.where(on_right, pltpu.roll(from_right, back, 1),
                         jnp.where(on_left, pltpu.roll(from_left, (back + nx - HALO) % nx, 1), 0.0))

    b = [jnp.concatenate([border_of(p, g) for g in range(-1, groups + 1)], axis=0) for p in range(PLANES)]

    def east(a, b):
        ra, rb = pltpu.roll(a, nx - 1, 1), pltpu.roll(b, nx - 1, 1)
        return jnp.where(elast, rb, ra), jnp.where(elast, ra, rb)

    def west(a, b):
        ra, rb = pltpu.roll(a, 1, 1), pltpu.roll(b, 1, 1)
        return jnp.where(efirst, rb, ra), jnp.where(efirst, ra, rb)

    mid = slice(HALO, HALO + rows)
    wests = west(a[3], b[3])
    terms = []
    for s, planes in enumerate((a, b)):
        there = planes[1] > 0.0
        inv = jnp.where(there, RELAX / jnp.where(there, planes[1], 1.0), 0.0)
        field[s, mid, :] = planes[2]
        south = field[s, HALO - 1:HALO - 1 + rows, :]
        terms.append((planes[0] * inv, planes[2] * inv, south * inv, planes[3] * inv, wests[s] * inv))

    c = [terms[0][0], terms[1][0]]
    for sweep in range(1, SWEEPS):
        e, ws = east(*c), west(*c)
        for s in range(2):
            field[s, mid, :] = c[s]
        nxt = []
        for s in range(2):
            r, tyn, tys, txe, txw = terms[s]
            nxt.append((1.0 - RELAX) * c[s] + r
                       + tyn * field[s, HALO + 1:HALO + 1 + rows, :] + tys * field[s, HALO - 1:HALO - 1 + rows, :]
                       + txe * e[s] + txw * ws[s])
        c = nxt
    e, ws = east(*c), west(*c)
    final[0] = c[0]
    final[1] = e[0]
    final[2] = ws[0]
    wait_send(halos + rest)
    for copy in sums:
        copy.wait_send()
    wait_send(coarse)


def finish_kernel(parts, w, qv, tzs, ty, txp, txm, final, new_hbm, corr_ref, out, out_sem):
    nz, ny, nx = tzs.shape
    own = slice(HALO, HALO + ny)
    cc, ce, cw = (final[k, own, :] for k in range(3))
    cn, cs = final[0, HALO + 1:HALO + 1 + ny, :], final[0, HALO - 1:HALO - 1 + ny, :]
    corr_ref[...] = cc

    def finish(z, _):
        g = (tzs[z] * cc + ty[z, own, :] * cn + ty[z, HALO - 1:HALO + ny - 1, :] * cs
             + txp[z] * ce + txm[z] * cw)
        for r in range(3):
            out[r, z] = w[r, z] + qv[r, z] * g
        return 0

    step = nz // parts
    outs = []
    for part in range(parts):
        lax.fori_loop(part * step, (part + 1) * step, finish, 0)
        chunk = slice(part * step, (part + 1) * step)
        outs.append(pltpu.make_async_copy(out.at[:, chunk], new_hbm.at[:, chunk], out_sem.at[part]))
        outs[-1].start()
    for copy in outs:
        copy.wait()


def per_device(sizes, state, right_side, permeability, pore_volume, facies, storage_table, coupling_table):
    _, nz, ny, nx = state.shape
    sizes = sizes + (nz, ny, nx)
    f32 = jnp.float32
    ngz = sizes[2]
    cells = (nz, ny, nx)
    vmem = lambda *shape: pltpu.VMEM(shape, f32)
    hbm = pl.BlockSpec(memory_space=pltpu.HBM)
    dma = lambda n: pltpu.SemaphoreType.DMA((n,))
    ey = ny + 2 * HALO
    split = upper_rows(ny)
    tiles = -(-(ny // HALO) // (nx // (PLANES * HALO)))
    facets = storage_table.shape[0]
    in_vmem = pl.BlockSpec(memory_space=pltpu.VMEM)
    handed = 4 * nx * (9 * nz * ny + nz * ey + 3 * ey)
    limit = 16384 * ((VMEM_BYTES - handed) // 16384)
    middle = pl.pallas_call(
        functools.partial(kernel, sizes),
        out_shape=(vmem(3, *cells), vmem(3, *cells), vmem(*cells), vmem(nz, ey, nx), vmem(*cells), vmem(*cells),
                   vmem(3, ey, nx)),
        in_specs=[hbm, hbm, hbm, hbm, hbm, hbm, hbm],
        out_specs=(in_vmem,) * 7,
        scratch_shapes=[
            vmem(4, nz + 2, ey, nx), vmem(3, *cells),
            pltpu.VMEM(cells, permeability.dtype), pltpu.VMEM(cells, pore_volume.dtype),
            vmem(2, 2, 2 * nz, nx), vmem(2, 2, 2 * nz, nx), vmem(2, split, nx), vmem(2, 2, split, nx),
            vmem(2, 4, ny, nx), vmem(2, 4 * nz, nx), vmem(nz, nx),
            vmem(3, *cells), vmem(*cells),
            vmem(ngz, PLANES, ny, nx), vmem(PLANES, ey, nx),
            vmem(2, tiles, HALO, nx), vmem(2, tiles, HALO, nx), vmem(2, 2, HALO, nx), vmem(2, ey + 2 * HALO, nx),
            pltpu.SMEM((nz,), facies.dtype), pltpu.SMEM((3, facets, 3), f32), pltpu.SMEM((3, facets, 3), f32),
            pltpu.SemaphoreType.REGULAR, dma(7), dma(10), dma(10), dma(max(ngz - 1, 1)), dma(ngz), dma(8), dma(8),
        ],
        compiler_params=pltpu.CompilerParams(collective_id=0, has_side_effects=True, vmem_limit_bytes=limit),
        name="cpr_apply",
    )(facies, storage_table.transpose(1, 0, 2), coupling_table.transpose(1, 0, 2),
      state, right_side, permeability, pore_volume)
    parts = 4
    return tuple(pl.pallas_call(
        functools.partial(finish_kernel, parts),
        out_shape=(jax.ShapeDtypeStruct(state.shape, f32), jax.ShapeDtypeStruct((ny, nx), f32)),
        in_specs=[in_vmem] * 7,
        out_specs=(hbm, in_vmem),
        scratch_shapes=[vmem(3, *cells), dma(parts)],
        compiler_params=pltpu.CompilerParams(vmem_limit_bytes=16 * 2**20),
        name="cpr_finish",
    )(*middle))


def solution(mesh):
    sizes = (mesh.shape["gx"], mesh.shape["gy"], mesh.shape["gz"])
    return jax.shard_map(
        functools.partial(per_device, sizes),
        mesh=mesh,
        in_specs=(
            P(None, "gz", "gy", "gx"),
            P(None, "gz", "gy", "gx"),
            P("gz", "gy", "gx"),
            P("gz", "gy", "gx"),
            P("gz"),
            P(),
            P(),
        ),
        out_specs=(P(None, "gz", "gy", "gx"), P("gy", "gx")),
        check_vma=False,
    )
```

```python
import functools
import jax
import jax.numpy as jnp
from jax import lax
from jax.experimental import pallas as pl
from jax.experimental.pallas import tpu as pltpu
from jax.sharding import PartitionSpec as P

SWEEPS = 8
RELAX = 0.8
MESH = pl.DeviceIdType.MESH
HALO = 8
VMEM_BYTES = 67043328

PLANES = 4
SIDES = [(-1, 0), (1, 0), (0, -1), (0, 1), (-1, -1), (-1, 1), (1, -1), (1, 1)]


def face(a, b):
    return 2.0 * a * b / (a + b)


def upper_rows(ny):
    return HALO * (-(-ny // (2 * HALO)))


def kernel(sizes, facies_hbm, mtab_hbm, ktab_hbm, state_hbm, rhs_hbm, perm_hbm, pore_hbm,
           w, qv, tzs, ty, txp, txm, final,
           u, rhs, permb, poreb, ysend, yrecv, xsend, xrecv, zrecv, yedge, rowk,
           flux, tot, zplanes, ext, cxsend, cxrecv, cdsend, cdrecv, field,
           facies, mtab, ktab, near_sem, far_sem, in_sem, h_send, h_recv, z_send, z_recv, c_send, c_recv, d_send, d_recv):
    ngx, ngy, ngz, nz, ny, nx = sizes
    ix, iy, iz = lax.axis_index("gx"), lax.axis_index("gy"), lax.axis_index("gz")
    own = slice(HALO, HALO + ny)
    split = upper_rows(ny)

    def exists(dy, dx):
        ok = None
        for d, i, n in ((dy, iy, ngy), (dx, ix, ngx)):
            if d:
                here = (i > 0) if d < 0 else (i < n - 1)
                ok = here if ok is None else jnp.logical_and(ok, here)
        return ok

    def at(dy, dx):
        return {"gx": ix + dx, "gy": iy + dy, "gz": iz}

    barrier = pltpu.get_barrier_semaphore()
    for side in SIDES[:4]:
        @pl.when(exists(*side))
        def _(side=side):
            pl.semaphore_signal(barrier, inc=1, device_id=at(*side), device_id_type=MESH)

    def signal_peers(sem):
        for d in range(1, ngz):
            pl.semaphore_signal(sem, inc=1, device_id={"gx": ix, "gy": iy, "gz": lax.rem(iz + d, ngz)},
                                device_id_type=MESH)

    signal_peers(barrier)

    loads = [
        pltpu.make_async_copy(perm_hbm, permb, in_sem.at[0]),
        pltpu.make_async_copy(state_hbm, u.at[0:3, 1:nz + 1, own], in_sem.at[1]),
        pltpu.make_async_copy(pore_hbm, poreb, in_sem.at[2]),
        pltpu.make_async_copy(rhs_hbm, rhs, in_sem.at[3]),
        pltpu.make_async_copy(facies_hbm, facies, in_sem.at[4]),
        pltpu.make_async_copy(mtab_hbm, mtab, in_sem.at[5]),
        pltpu.make_async_copy(ktab_hbm, ktab, in_sem.at[6]),
    ]
    for load in loads:
        load.start()

    lane = lax.broadcasted_iota(jnp.int32, (ny, nx), 1)

    def zero(ref):
        ref[...] = jnp.zeros(ref.shape, ref.dtype)

    for cond, refs in (
        (iz == 0, [zrecv.at[0]]),
        (iz == ngz - 1, [zrecv.at[1]]),
        (iy == 0, [yrecv.at[:, 0], ext.at[:, 0:HALO]]),
        (iy == ngy - 1, [yrecv.at[:, 1], ext.at[:, HALO + ny:]]),
        (ix == 0, [xrecv.at[:, 0], cxrecv.at[0]]),
        (ix == ngx - 1, [xrecv.at[:, 1], cxrecv.at[1]]),
        (jnp.logical_or(iy == 0, ix == 0), [cdrecv.at[:, 0, 0]]),
        (jnp.logical_or(iy == 0, ix == ngx - 1), [cdrecv.at[:, 0, 1]]),
        (jnp.logical_or(iy == ngy - 1, ix == 0), [cdrecv.at[:, 1, 0]]),
        (jnp.logical_or(iy == ngy - 1, ix == ngx - 1), [cdrecv.at[:, 1, 1]]),
    ):
        @pl.when(cond)
        def _(refs=refs):
            for ref in refs:
                zero(ref)
    zero(field)
    zero(u.at[:, nz + 1, own])
    zero(u.at[:, 0, own])

    loads[0].wait()
    for load in loads[4:]:
        load.wait()

    def loop(begin, end, body, carry, unroll):
        def several(i, carry):
            for k in range(unroll):
                carry = body(begin + i * unroll + k, carry)
            return carry
        return lax.fori_loop(0, (end - begin) // unroll, several, carry)

    def coefficient(table, z, r, c):
        return table[r, facies[z], c]

    def widen(z, _):
        u[3, z + 1, own, :] = permb[z].astype(jnp.float32)
        for k in range(4):
            u[k, z + 1, 0:HALO, :] = jnp.zeros((HALO, nx), jnp.float32)
            u[k, z + 1, HALO + ny:, :] = jnp.zeros((HALO, nx), jnp.float32)
        rowk[pl.ds(z, 1), :] = jnp.full((1, nx), coefficient(ktab, z, 0, 0), jnp.float32)
        return 0

    loop(0, nz, widen, 0, 2)
    loads[1].wait()

    def pair(batch, z, part):
        if batch:
            return part(1), part(2)
        return sum(coefficient(ktab, z, 0, k) * part(k) for k in range(3)), part(3)

    def pack_rows(batch):
        def body(z, _):
            for side, at_row in ((0, HALO), (1, HALO + ny - 1)):
                for i, x in enumerate(pair(batch, z, lambda k: u[k, z + 1, at_row:at_row + 1, :])):
                    ysend[batch, side, pl.ds(i * nz + z, 1), :] = x
            return 0

        loop(0, nz, body, 0, 4)

    pack_rows(0)

    count = sum(exists(*side).astype(jnp.int32) for side in SIDES[:4])
    pl.semaphore_wait(barrier, count + (ngz - 1))
    for side in SIDES[:4]:
        @pl.when(exists(*side))
        def _(side=side):
            pl.semaphore_signal(near_sem, inc=1, device_id=at(*side), device_id_type=MESH)
    signal_peers(near_sem)

    def remote(src, dst, send, recv, device):
        return pltpu.make_async_remote_copy(src_ref=src, dst_ref=dst, send_sem=send, recv_sem=recv,
                                            device_id=device, device_id_type=MESH)

    def z_device(d):
        return {"gx": ix, "gy": iy, "gz": iz + d}

    halos = [
        (iz < ngz - 1, iz > 0, remote(u.at[:, nz, own], zrecv.at[0], h_send.at[0], h_recv.at[0], z_device(1))),
        (iz > 0, iz < ngz - 1, remote(u.at[:, 1, own], zrecv.at[1], h_send.at[1], h_recv.at[1], z_device(-1))),
        (exists(1, 0), exists(-1, 0), remote(ysend.at[0, 1], yrecv.at[0, 0], h_send.at[2], h_recv.at[2], at(1, 0))),
        (exists(-1, 0), exists(1, 0), remote(ysend.at[0, 0], yrecv.at[0, 1], h_send.at[3], h_recv.at[3], at(-1, 0))),
        (exists(0, 1), exists(0, -1), remote(xsend.at[0], xrecv.at[0, 0], h_send.at[4], h_recv.at[4], at(0, 1))),
        (exists(0, -1), exists(0, 1), remote(xsend.at[0], xrecv.at[0, 1], h_send.at[5], h_recv.at[5], at(0, -1))),
    ]
    rest = [
        (exists(1, 0), exists(-1, 0), remote(ysend.at[1, 1], yrecv.at[1, 0], h_send.at[6], h_recv.at[6], at(1, 0))),
        (exists(-1, 0), exists(1, 0), remote(ysend.at[1, 0], yrecv.at[1, 1], h_send.at[7], h_recv.at[7], at(-1, 0))),
        (exists(0, 1), exists(0, -1), remote(xsend.at[1], xrecv.at[1, 0], h_send.at[8], h_recv.at[8], at(0, 1))),
        (exists(0, -1), exists(0, 1), remote(xsend.at[1], xrecv.at[1, 1], h_send.at[9], h_recv.at[9], at(0, -1))),
    ]

    def start(copies):
        for sends, _, copy in copies:
            @pl.when(sends)
            def _(copy=copy):
                copy.start()

    def wait_recv(copies):
        for _, gets, copy in copies:
            @pl.when(gets)
            def _(copy=copy):
                copy.wait_recv()

    def wait_send(copies):
        for sends, _, copy in copies:
            @pl.when(sends)
            def _(copy=copy):
                copy.wait_send()

    start(halos[:4])

    half = nx // 2
    lane_pair = lax.shift_right_logical(lane, 1)
    nil = jnp.zeros((ny, nx), jnp.float32)

    def pack_columns(batch):
        def body(z, carry):
            packed, lanek = carry
            for i, x in enumerate(pair(batch, z, lambda k: u[k, z + 1, own, :])):
                j = i * nz + z
                upper = pltpu.roll(x[:split], 2 * j + 1, 1)
                lower = pltpu.roll(x[split:], lax.rem(2 * j + 1 + half, nx), 1)
                packed = jnp.where(lane_pair[:split] == j, upper, packed)
                beside = jnp.where(lane_pair[:ny - split] == j + half // 2, lower, packed[:ny - split])
                packed = beside if ny == 2 * split else jnp.concatenate([beside, packed[ny - split:]], axis=0)
            lanek = jnp.where(lane_pair[0:1] == nz + z, coefficient(ktab, z, 0, 0), lanek)
            return packed, lanek

        packed, lanek = loop(0, nz, body, (nil[:split], nil[0:1]), 4)
        xsend[batch] = packed
        return lanek

    def unpacked(x):
        return jnp.concatenate([x, pltpu.roll(x[:ny - split], half, 1)], axis=0)

    lanek = pack_columns(0)
    start(halos[4:])
    pack_rows(1)
    pack_columns(1)
    start(rest)
    loads[2].wait()
    loads[3].wait()

    first, last = lane == 0, lane == nx - 1

    def assemble(z, carry):
        tzm, s_rhs, s_diag, s_ty, s_tx = carry
        q = u[3, z + 1, own, :]
        tzp = face(q, u[3, z + 2, own, :])
        typ = face(q, u[3, z + 1, HALO + 1:HALO + ny + 1, :])
        ty[z, own, :] = typ
        ty[z, 0:HALO, :] = jnp.zeros((HALO, nx), jnp.float32)
        tym = ty[z, HALO - 1:HALO + ny - 1, :]
        xp = jnp.where(last, 0.0, face(q, pltpu.roll(q, nx - 1, 1)))
        xm = pltpu.roll(xp, 1, 1)
        txp[z] = xp
        txm[z] = xm
        tz = tzp + tzm
        areal = typ + tym + xp + xm
        tzs[z] = tz
        tot[z] = tz + areal
        v = poreb[z].astype(jnp.float32)
        local, moved = 0.0, 0.0
        for k in range(3):
            c = u[k, z + 1, own, :]
            f = (tzp * (c - u[k, z + 2, own, :]) + tzm * (c - u[k, z, own, :])
                 + typ * (c - u[k, z + 1, HALO + 1:HALO + ny + 1, :])
                 + tym * (c - u[k, z + 1, HALO - 1:HALO + ny - 1, :])
                 + xp * (c - pltpu.roll(c, nx - 1, 1)) + xm * (c - pltpu.roll(c, 1, 1)))
            flux[k, z] = f
            local = local + coefficient(mtab, z, 0, k) * c
            moved = moved + coefficient(ktab, z, 0, k) * f
        res = rhs[0, z] - (v * local + moved)
        k00 = coefficient(ktab, z, 0, 0)
        return (tzp, s_rhs + res, s_diag + (v * coefficient(mtab, z, 0, 0) + k00 * areal),
                s_ty + k00 * typ, s_tx + k00 * xp)

    _, s_rhs, s_diag, s_ty, s_tx = loop(0, nz, assemble, (nil,) * 5, 2)
    pl.semaphore_wait(near_sem, count + (ngz - 1))
    signal_peers(far_sem)
    wait_recv(halos)

    for side, z in ((0, 0), (1, nz - 1)):
        t = face(u[3, z + 1, own, :], zrecv[side, 3])
        for k in range(3):
            f = t * (u[k, z + 1, own, :] - zrecv[side, k])
            flux[k, z] = flux[k, z] + f
            s_rhs = s_rhs - coefficient(ktab, z, 0, k) * f
        tzs[z] = tzs[z] + t
        tot[z] = tot[z] + t

    row = lax.broadcasted_iota(jnp.int32, (ny, nx), 0)
    for side, at_row in ((0, 0), (1, ny - 1)):
        t = face(ysend[0, side, nz:, :], yrecv[0, side, nz:, :])
        f = t * (ysend[0, side, :nz, :] - yrecv[0, side, :nz, :])
        yedge[side, 0:nz, :] = f
        yedge[side, 3 * nz:, :] = t
        moved = jnp.sum(f, axis=0, keepdims=True)
        weight = jnp.sum(rowk[...] * t, axis=0, keepdims=True)
        here = row == at_row
        s_rhs = s_rhs - jnp.where(here, moved, 0.0)
        s_diag = s_diag + jnp.where(here, weight, 0.0)
        if side:
            s_ty = s_ty + jnp.where(here, weight, 0.0)

    even = lax.rem(lane, 2) == 0
    low_at = jnp.logical_and(even, lane < 2 * nz)
    high_at = jnp.logical_and(even, jnp.logical_and(lane >= 2 * nz, lane < 4 * nz))

    def columns(batch, side):
        mine, other = unpacked(xsend[batch]), unpacked(xrecv[batch, side])
        if side:
            return mine, pltpu.roll(other, nx - 1, 1)
        return pltpu.roll(mine, nx - 1, 1), other

    def merged(edges):
        return jnp.where(even, edges[0], pltpu.roll(edges[1], nx - 1, 1))

    edges, spread = [], []
    for side, edge in ((0, first), (1, last)):
        here, there = columns(0, side)
        t = jnp.where(high_at, face(jnp.where(high_at, here, 1.0), jnp.where(high_at, there, 1.0)), 0.0)
        down = pltpu.roll(t, nx - 2 * nz, 1)
        f = jnp.where(low_at, down * (here - there), 0.0)
        moved = jnp.sum(f, axis=1, keepdims=True)
        weight = jnp.sum(t * lanek, axis=1, keepdims=True)
        s_rhs = s_rhs - jnp.where(edge, moved, 0.0)
        s_diag = s_diag + jnp.where(edge, weight, 0.0)
        if side:
            s_tx = s_tx + jnp.where(edge, weight, 0.0)
        edges.append(f + t)
        spread.append(down + t)
    border = merged(edges)

    for p, plane in enumerate((s_rhs, s_diag, s_ty, s_tx)):
        zplanes[iz, p] = plane

    slots = nx // (PLANES * HALO)
    groups = ny // HALO
    lane_group = lax.shift_right_logical(lane[:HALO], 3)
    for v, g in ((0, 0), (1, groups - 1)):
        packed = [nil[:HALO]] * 2
        for p, plane in enumerate((s_rhs, s_diag, s_ty, s_tx)):
            for side, shift in ((0, p * HALO), (1, (p + 1) * HALO)):
                packed[side] = jnp.where(lane_group == p, pltpu.roll(plane[g * HALO:(g + 1) * HALO], shift % nx, 1),
                                         packed[side])
        for side in range(2):
            cdsend[v, side] = packed[side]
    pl.semaphore_wait(far_sem, ngz - 1)
    corners, arrivals = [], []
    for n, (dy, dx) in enumerate(SIDES[4:]):
        src, into = cdsend.at[(dy + 1) // 2, (dx + 1) // 2], ((1 - dy) // 2, (1 - dx) // 2)
        for d in range(ngz):
            device = {"gx": ix + dx, "gy": iy + dy, "gz": lax.rem(iz + d, ngz)}
            corners.append((exists(dy, dx), None,
                            remote(src, cdrecv.at[iz, into[0], into[1]], d_send.at[n * ngz + d], d_recv.at[n * ngz + iz], device)))
            arrivals.append((None, exists(-dy, -dx),
                             remote(src, cdrecv.at[d, into[0], into[1]], d_send.at[n * ngz + d], d_recv.at[n * ngz + d], device)))
    start(corners)

    others = [lax.rem(iz + d, ngz) for d in range(1, ngz)]
    sums = [remote(zplanes.at[iz], zplanes.at[iz], z_send.at[d], z_recv.at[iz], {"gx": ix, "gy": iy, "gz": peer})
            for d, peer in enumerate(others)]
    for copy in sums:
        copy.start()

    outer = jnp.logical_or(first, last)

    def solve(z, _):
        v = poreb[z].astype(jnp.float32)
        k01, k02 = coefficient(ktab, z, 0, 1), coefficient(ktab, z, 0, 2)
        inv_k00 = 1.0 / rowk[pl.ds(z, 1), :]
        for side, at_row in ((0, 0), (1, ny - 1)):
            here = slice(at_row, at_row + 1)
            coarse_row, one, two, t = (yedge[side, pl.ds(k * nz + z, 1), :] for k in range(4))
            zero_row = (coarse_row - k01 * one - k02 * two) * inv_k00
            for k, x in enumerate((zero_row, one, two)):
                flux[k, z, here, :] = flux[k, z, here, :] + x
            tot[z, here, :] = tot[z, here, :] + t
            at_face = HALO - 1 + side * ny
            ty[z, at_face:at_face + 1, :] = t

        def beside(values, j):
            return jnp.where(outer, pltpu.roll(values, lax.rem(2 * nx - 2 * j, nx), 1), 0.0)

        one, two = beside(border_rest, z), beside(border_rest, nz + z)
        added = [(beside(border, z) - k01 * one - k02 * two) * inv_k00, one, two]
        t = beside(border, nz + z)
        txp[z] = txp[z] + jnp.where(last, t, 0.0)
        txm[z] = txm[z] + jnp.where(first, t, 0.0)
        total = tot[z] + t
        m = [[coefficient(mtab, z, r, c) for c in range(3)] for r in range(3)]
        kk = [[coefficient(ktab, z, r, c) for c in range(3)] for r in range(3)]
        e = [[v * m[r][c] + total * kk[r][c] for c in range(3)] for r in range(3)]

        def cofactor(r, c):
            return (e[(r + 1) % 3][(c + 1) % 3] * e[(r + 2) % 3][(c + 2) % 3]
                    - e[(r + 1) % 3][(c + 2) % 3] * e[(r + 2) % 3][(c + 1) % 3])

        cells = [u[k, z + 1, own, :] for k in range(3)]
        f = [flux[k, z] + added[k] for k in range(3)]
        res = []
        for r in range(3):
            res.append(rhs[r, z] - (v * (m[r][0] * cells[0] + m[r][1] * cells[1] + m[r][2] * cells[2])
                                    + (kk[r][0] * f[0] + kk[r][1] * f[1] + kk[r][2] * f[2])))
        fac = [[cofactor(r, c) for c in range(3)] for r in range(3)]
        inv = 1.0 / (e[0][0] * fac[0][0] + e[0][1] * fac[0][1] + e[0][2] * fac[0][2])
        for r in range(3):
            w[r, z] = cells[r] + (fac[0][r] * res[0] + fac[1][r] * res[1] + fac[2][r] * res[2]) * inv
            qv[r, z] = (fac[0][r] * kk[0][0] + fac[1][r] * kk[1][0] + fac[2][r] * kk[2][0]) * inv
        return 0

    for peer in others:
        remote(zplanes.at[peer], zplanes.at[peer], z_send.at[0], z_recv.at[peer],
               {"gx": ix, "gy": iy, "gz": peer}).wait_recv()
    tiles = cxsend.shape[1]
    packed = [[nil[:HALO]] * tiles for _ in range(2)]
    for p in range(PLANES):
        plane = zplanes[0, p]
        for i in range(1, ngz):
            plane = plane + zplanes[i, p]
        ext[p, own, :] = plane
        for g in range(groups):
            slot = (g % slots) * PLANES + p
            for side, shift in ((0, slot * HALO), (1, (slot + 1) * HALO)):
                moved = pltpu.roll(plane[g * HALO:(g + 1) * HALO], shift % nx, 1)
                packed[side][g // slots] = jnp.where(lane_group == slot, moved, packed[side][g // slots])
    for side in range(2):
        for tile in range(tiles):
            cxsend[side, tile] = packed[side][tile]

    low, high = slice(0, HALO), slice(ny - HALO, ny)
    elow, ehigh = slice(0, HALO), slice(HALO + ny, 2 * HALO + ny)
    coarse = []
    for s, (dy, dx) in enumerate(SIDES[:4]):
        rows = low if dy < 0 else high
        into = ehigh if dy < 0 else elow
        if dx == 0:
            src, dst = ext.at[:, slice(rows.start + HALO, rows.stop + HALO)], ext.at[:, into]
        else:
            src, dst = cxsend.at[(dx + 1) // 2], cxrecv.at[(1 - dx) // 2]
        coarse.append((exists(dy, dx), exists(-dy, -dx), remote(src, dst, c_send.at[s], c_recv.at[s], at(dy, dx))))
    start(coarse)
    wait_recv(rest)
    for side in range(2):
        t = yedge[side, 3 * nz:, :]
        for i in range(2):
            part = slice(i * nz, (i + 1) * nz)
            yedge[side, (i + 1) * nz:(i + 2) * nz, :] = t * (ysend[1, side, part, :] - yrecv[1, side, part, :])
    edges = []
    for side in range(2):
        here, there = columns(1, side)
        edges.append(jnp.where(lane < 4 * nz, spread[side] * (here - there), 0.0))
    border_rest = merged(edges)
    loop(0, nz, solve, 0, 2)
    wait_recv(coarse)
    wait_recv(arrivals)

    rows = ny + 2 * HALO
    elane = lax.broadcasted_iota(jnp.int32, (rows, nx), 1)
    efirst, elast = elane == 0, elane == nx - 1
    a = [ext[p] for p in range(PLANES)]
    on_right, on_left = lane[:HALO] < HALO, lane[:HALO] >= nx - HALO

    corner = [[cdrecv[0, v, side] for side in range(2)] for v in range(2)]
    for i in range(1, ngz):
        corner = [[corner[v][side] + cdrecv[i, v, side] for side in range(2)] for v in range(2)]

    def border_of(p, g):
        if 0 <= g < groups:
            slot = (g % slots) * PLANES + p
            from_left, from_right = cxrecv[0, g // slots], cxrecv[1, g // slots]
        else:
            slot = p
            from_left, from_right = corner[0 if g < 0 else 1]
        back = (nx - slot * HALO) % nx
        return jnp.where(on_right, pltpu.roll(from_right, back, 1),
                         jnp.where(on_left, pltpu.roll(from_left, (back + nx - HALO) % nx, 1), 0.0))

    b = [jnp.concatenate([border_of(p, g) for g in range(-1, groups + 1)], axis=0) for p in range(PLANES)]

    def east(a, b):
        ra, rb = pltpu.roll(a, nx - 1, 1), pltpu.roll(b, nx - 1, 1)
        return jnp.where(elast, rb, ra), jnp.where(elast, ra, rb)

    def west(a, b):
        ra, rb = pltpu.roll(a, 1, 1), pltpu.roll(b, 1, 1)
        return jnp.where(efirst, rb, ra), jnp.where(efirst, ra, rb)

    mid = slice(HALO, HALO + rows)
    wests = west(a[3], b[3])
    terms = []
    for s, planes in enumerate((a, b)):
        there = planes[1] > 0.0
        inv = jnp.where(there, RELAX / jnp.where(there, planes[1], 1.0), 0.0)
        field[s, mid, :] = planes[2]
        south = field[s, HALO - 1:HALO - 1 + rows, :]
        terms.append((planes[0] * inv, planes[2] * inv, south * inv, planes[3] * inv, wests[s] * inv))

    c = [terms[0][0], terms[1][0]]
    for sweep in range(1, SWEEPS):
        e, ws = east(*c), west(*c)
        for s in range(2):
            field[s, mid, :] = c[s]
        nxt = []
        for s in range(2):
            r, tyn, tys, txe, txw = terms[s]
            nxt.append((1.0 - RELAX) * c[s] + r
                       + tyn * field[s, HALO + 1:HALO + 1 + rows, :] + tys * field[s, HALO - 1:HALO - 1 + rows, :]
                       + txe * e[s] + txw * ws[s])
        c = nxt
    e, ws = east(*c), west(*c)
    final[0] = c[0]
    final[1] = e[0]
    final[2] = ws[0]
    wait_send(halos + rest)
    for copy in sums:
        copy.wait_send()
    wait_send(coarse)
    wait_send(corners)


def finish_kernel(parts, w, qv, tzs, ty, txp, txm, final, new_hbm, corr_ref, out, out_sem):
    nz, ny, nx = tzs.shape
    own = slice(HALO, HALO + ny)
    cc, ce, cw = (final[k, own, :] for k in range(3))
    cn, cs = final[0, HALO + 1:HALO + 1 + ny, :], final[0, HALO - 1:HALO - 1 + ny, :]
    corr_ref[...] = cc

    def finish(z, _):
        g = (tzs[z] * cc + ty[z, own, :] * cn + ty[z, HALO - 1:HALO + ny - 1, :] * cs
             + txp[z] * ce + txm[z] * cw)
        for r in range(3):
            out[r, z] = w[r, z] + qv[r, z] * g
        return 0

    step = nz // parts
    outs = []
    for part in range(parts):
        lax.fori_loop(part * step, (part + 1) * step, finish, 0)
        chunk = slice(part * step, (part + 1) * step)
        outs.append(pltpu.make_async_copy(out.at[:, chunk], new_hbm.at[:, chunk], out_sem.at[part]))
        outs[-1].start()
    for copy in outs:
        copy.wait()


def per_device(sizes, state, right_side, permeability, pore_volume, facies, storage_table, coupling_table):
    _, nz, ny, nx = state.shape
    sizes = sizes + (nz, ny, nx)
    f32 = jnp.float32
    ngz = sizes[2]
    cells = (nz, ny, nx)
    vmem = lambda *shape: pltpu.VMEM(shape, f32)
    hbm = pl.BlockSpec(memory_space=pltpu.HBM)
    dma = lambda n: pltpu.SemaphoreType.DMA((n,))
    ey = ny + 2 * HALO
    split = upper_rows(ny)
    tiles = -(-(ny // HALO) // (nx // (PLANES * HALO)))
    facets = storage_table.shape[0]
    in_vmem = pl.BlockSpec(memory_space=pltpu.VMEM)
    handed = 4 * nx * (9 * nz * ny + nz * ey + 3 * ey)
    limit = 16384 * ((VMEM_BYTES - handed) // 16384)
    middle = pl.pallas_call(
        functools.partial(kernel, sizes),
        out_shape=(vmem(3, *cells), vmem(3, *cells), vmem(*cells), vmem(nz, ey, nx), vmem(*cells), vmem(*cells),
                   vmem(3, ey, nx)),
        in_specs=[hbm, hbm, hbm, hbm, hbm, hbm, hbm],
        out_specs=(in_vmem,) * 7,
        scratch_shapes=[
            vmem(4, nz + 2, ey, nx), vmem(3, *cells),
            pltpu.VMEM(cells, permeability.dtype), pltpu.VMEM(cells, pore_volume.dtype),
            vmem(2, 2, 2 * nz, nx), vmem(2, 2, 2 * nz, nx), vmem(2, split, nx), vmem(2, 2, split, nx),
            vmem(2, 4, ny, nx), vmem(2, 4 * nz, nx), vmem(nz, nx),
            vmem(3, *cells), vmem(*cells),
            vmem(ngz, PLANES, ny, nx), vmem(PLANES, ey, nx),
            vmem(2, tiles, HALO, nx), vmem(2, tiles, HALO, nx), vmem(2, 2, HALO, nx), vmem(ngz, 2, 2, HALO, nx), vmem(2, ey + 2 * HALO, nx),
            pltpu.SMEM((nz,), facies.dtype), pltpu.SMEM((3, facets, 3), f32), pltpu.SMEM((3, facets, 3), f32),
            pltpu.SemaphoreType.REGULAR, pltpu.SemaphoreType.REGULAR, dma(7), dma(10), dma(10), dma(max(ngz - 1, 1)), dma(ngz), dma(4), dma(4), dma(4 * ngz), dma(4 * ngz),
        ],
        compiler_params=pltpu.CompilerParams(collective_id=0, has_side_effects=True, vmem_limit_bytes=limit),
        name="cpr_apply",
    )(facies, storage_table.transpose(1, 0, 2), coupling_table.transpose(1, 0, 2),
      state, right_side, permeability, pore_volume)
    parts = 4
    return tuple(pl.pallas_call(
        functools.partial(finish_kernel, parts),
        out_shape=(jax.ShapeDtypeStruct(state.shape, f32), jax.ShapeDtypeStruct((ny, nx), f32)),
        in_specs=[in_vmem] * 7,
        out_specs=(hbm, in_vmem),
        scratch_shapes=[vmem(3, *cells), dma(parts)],
        compiler_params=pltpu.CompilerParams(vmem_limit_bytes=16 * 2**20),
        name="cpr_finish",
    )(*middle))


def solution(mesh):
    sizes = (mesh.shape["gx"], mesh.shape["gy"], mesh.shape["gz"])
    return jax.shard_map(
        functools.partial(per_device, sizes),
        mesh=mesh,
        in_specs=(
            P(None, "gz", "gy", "gx"),
            P(None, "gz", "gy", "gx"),
            P("gz", "gy", "gx"),
            P("gz", "gy", "gx"),
            P("gz"),
            P(),
            P(),
        ),
        out_specs=(P(None, "gz", "gy", "gx"), P("gy", "gx")),
        check_vma=False,
    )
```
